32 devices in a mesh: mem: 4 (over z), gx: 4 (over y, core), gy: 2 (over x).
Axes of the slice: x: 2, y: 2, z: 4, core: 2. Of those that a mesh axis runs over, the one named last changes fastest.
Arguments:
- height: float32 [4, 4, 128, 256], P('mem', None, 'gx', 'gy'), may hold values from -4 to 4
- wind: float32 [4, 2, 4, 128, 256], P('mem', None, None, 'gx', 'gy'), may hold values from -0.8 to 0.8
- moisture: float32 [4, 4, 128, 256], P('mem', None, 'gx', 'gy'), may hold values from 0 to 2
- coeffs: float32 [4, 4, 4, 16384], P('mem', None, None, ('gx', 'gy')), may hold values from -6 to 6
- damping: float32 [16384], P(('gx', 'gy')), may hold values from 0.3 to 1
- vmix: float32 [4, 4], replicated, may hold values from -3 to 3
- basis: bfloat16 [16384, 384], P(('gx', 'gy')), may hold values from -0.046875 to 0.046875
- edge_source: int32 [768], replicated, may hold values from 0 to 383
- row_cell: int32 [128], replicated, may hold values from 0 to 15, never falling along the last dimension, each value on 1 to 16 neighbouring positions
- col_cell: int32 [256], replicated, may hold values from 0 to 31, never falling along the last dimension, each value on 1 to 16 neighbouring positions
- cond_rate: float32 [4], replicated, may hold values from 0.05 to 0.5
- saturation: float32 [4], replicated, may hold values from 0.5 to 1.5
- ancestry: int32 [4], replicated, may hold values from 0 to 3
Outputs:
- height_out: float32 [4, 4, 128, 256], P('mem', None, 'gx', 'gy')
- wind_out: float32 [4, 2, 4, 128, 256], P('mem', None, None, 'gx', 'gy')
- moisture_out: float32 [4, 4, 128, 256], P('mem', None, 'gx', 'gy')
- rainfall: float32 [4, 128, 256], P('mem', 'gx', 'gy')
- restricted: float32 [4, 4, 16, 32], P('mem')
- coeffs_out: float32 [4, 4, 4, 16384], P('mem', None, None, ('gx', 'gy'))
The draws below stay inside these ranges and needn't reach their ends.
Inputs may be any that keep to these rules, and one draw needn't show every extreme that they name: row_cell never falls, and each of the 16 global rows holds 1 to 16 nest rows, one exactly 16. col_cell never falls, and each of the 32 global columns holds 1 to 16 nest columns, one exactly 16.
All inputs are finite; a program needn't handle non-finite values.
Results may differ from the reference program's by a relative error of at most 0.00035.
Values sent between devices are 32-bit elements; how exact they have to be, the bound alone decides.
A program may use at most 64 MiB of HBM per device.

```python
import math
import jax
import jax.numpy as jnp
import numpy as np
from jax import lax

LEV = 4
RATIO = 8
RIM_G = 384
NSTEP = 1
ACOUSTIC = 2
MEMBERS = 4
NX = 128
NY = 256
KSPEC = 16384
GRX = 16
GRY = 32


def plant(entries, own_key, smallest, top_value):
    longest = entries.shape.index(max(entries.shape))
    spots = []
    for shift in (0, 1):
        where = [jax.random.randint(jax.random.fold_in(own_key, axis), (), 0, length) for axis, length in enumerate(entries.shape)]
        where[longest] = (where[longest] + shift) % entries.shape[longest]
        spots.append(tuple(where))
    return entries.at[spots[0]].set(smallest).at[spots[1]].set(top_value)


def shard_levels(own_key, extent, cuts, smallest, largest):
    level, own = 1.0, jax.random.fold_in(own_key, 6)
    for axis_at, shards_of in cuts:
        draws = jnp.exp(jax.random.uniform(jax.random.fold_in(own, axis_at), (shards_of,), jnp.float32, smallest / len(cuts), largest / len(cuts)))
        level = level * jnp.repeat(draws, extent[axis_at] // shards_of).reshape([-1 if axis == axis_at else 1 for axis in range(len(extent))])
    return level


def length_profile(number_of, total, most, skew):
    weights = [(1 << 20) // math.isqrt(rank ** skew) + 1 for rank in range(2, number_of + 1)]
    surplus, counts = total - most - (number_of - 1), [1] * (number_of - 1)
    while surplus > 0:
        movable = [i for i in range(number_of - 1) if counts[i] < most]
        pool, remaining = sum([weights[i] for i in movable]), surplus
        for i in movable:
            extra = min(most - counts[i], max(1, remaining * weights[i] // pool), surplus)
            counts[i] = counts[i] + extra
            surplus = surplus - extra
    return np.array([most] + counts)


def uneven_parts(stream_key, number_of, total, most, slope):
    if number_of == 2:
        one = jax.random.randint(stream_key, (), max(1, total - most), min(most, total - 1) + 1)
        return jnp.stack([one, total - one])
    tallies = jnp.asarray(length_profile(number_of, total, most, slope), jnp.int32)
    twos = (number_of - 1) // 2
    donor, receiver = tallies[1:1 + 2 * twos:2], tallies[2:2 + 2 * twos:2]
    room = jnp.minimum(donor - 1, most - receiver)
    shifted = jax.random.randint(jax.random.fold_in(stream_key, 1), (twos,), 0, 1 << 20) % (room + 1)
    tallies = tallies.at[1:1 + 2 * twos:2].set(donor - shifted).at[2:2 + 2 * twos:2].set(receiver + shifted)
    return tallies[jax.random.permutation(jax.random.fold_in(stream_key, 2), number_of)]


def centred(own_key, dims, scale, limit, shards=(), kind=jnp.bfloat16):
    entries = jax.random.normal(own_key, dims, jnp.float32) * scale
    if len(shards) > 0:
        entries = shard_levels(own_key, dims, shards, -0.22, 0.18) * entries
    return jnp.clip(entries, min=-limit, max=limit).astype(kind)


def setup_inputs(seed: int = 0) -> dict:
    key_of = jax.random.split(jax.random.key(seed), 14)
    height = centred(key_of[0], (MEMBERS, LEV, NX, NY), 1.0, 4.0, ((0, 4), (2, 4), (3, 2)), jnp.float32)
    wind = jnp.clip(jax.random.uniform(key_of[1], (MEMBERS, 2, LEV, NX, NY), jnp.float32, -0.8, 0.8) * shard_levels(key_of[1], (MEMBERS, 2, LEV, NX, NY), ((0, 4), (3, 4), (4, 2)), -0.4, 0.0), -0.8, 0.8)
    moisture = jnp.clip(2.0 * jax.random.uniform(key_of[2], (MEMBERS, LEV, NX, NY), jnp.float32) ** shard_levels(key_of[2], (MEMBERS, LEV, NX, NY), ((0, 4), (2, 4), (3, 2)), -0.2, 0.2), 0.0, 2.0)
    coeffs = centred(key_of[3], (MEMBERS, 4, LEV, KSPEC), 1.0, 6.0, ((0, 4), (3, 8)), jnp.float32)
    damping = jnp.clip(jnp.exp(math.log(1.0) - 1.2039728 * jax.random.uniform(key_of[4], (KSPEC,), jnp.float32) ** shard_levels(key_of[4], (KSPEC,), ((0, 8),), -0.2, 0.2)), 0.3, 1.0)
    vmix = centred(key_of[5], (LEV, LEV), LEV ** -0.5, 3.0, (), jnp.float32)
    basis = centred(key_of[6], (KSPEC, RIM_G), KSPEC ** -0.5, 0.046875, ((0, 8),))
    edge_source = plant(jax.random.randint(key_of[7], (2 * NX + 2 * NY,), 0, RIM_G), jax.random.fold_in(key_of[7], 1), 0, RIM_G - 1).astype(jnp.int32)
    row_cell = jnp.searchsorted(jnp.cumsum(uneven_parts(key_of[8], GRX, NX, 2 * RATIO, 0)), jnp.arange(NX), side="right").astype(jnp.int32)
    col_cell = jnp.searchsorted(jnp.cumsum(uneven_parts(key_of[9], GRY, NY, 2 * RATIO, 0)), jnp.arange(NY), side="right").astype(jnp.int32)
    cond_rate = jnp.clip(jnp.exp(jax.random.uniform(key_of[10], (LEV,), jnp.float32, math.log(0.05), math.log(0.5))), 0.05, 0.5)
    saturation = jnp.clip(jax.random.uniform(key_of[11], (LEV,), jnp.float32, 0.5, 1.5), 0.5, 1.5)
    ancestry = plant(jax.random.randint(key_of[12], (MEMBERS,), 0, MEMBERS), jax.random.fold_in(key_of[12], 1), 0, MEMBERS - 1).astype(jnp.int32)
    return dict(height=height, wind=wind, moisture=moisture, coeffs=coeffs, damping=damping, vmix=vmix, basis=basis, edge_source=edge_source, row_cell=row_cell, col_cell=col_cell, cond_rate=cond_rate, saturation=saturation, ancestry=ancestry)


acoustic_substep = 0.2
drift_step = 0.4


def framed_field(field, western_edge, eastern_edge, southern_edge, northern_edge):
    padded = jnp.pad(field, ((0, 0), (1, 1), (1, 1)))
    padded = padded.at[:, 0, 1:-1].set(western_edge)
    padded = padded.at[:, -1, 1:-1].set(eastern_edge)
    padded = padded.at[:, 1:-1, 0].set(southern_edge)
    padded = padded.at[:, 1:-1, -1].set(northern_edge)
    return padded


def member_run(height, uwind, meridional_wind, moist, western_edge, eastern_edge, southern_edge, northern_edge, cond_rate, saturation):
    rain = jnp.zeros(height.shape[1:], jnp.float32)
    for step in range(NSTEP):
        for substep in range(ACOUSTIC):
            hpad = framed_field(height, western_edge[0], eastern_edge[0], southern_edge[0], northern_edge[0])
            uwind = uwind - acoustic_substep * (hpad[:, 2:, 1:-1] - hpad[:, :-2, 1:-1])
            meridional_wind = meridional_wind - acoustic_substep * (hpad[:, 1:-1, 2:] - hpad[:, 1:-1, :-2])
            zonal_wind_padded = framed_field(uwind, western_edge[1], eastern_edge[1], southern_edge[1], northern_edge[1])
            meridional_wind_padded = framed_field(meridional_wind, western_edge[2], eastern_edge[2], southern_edge[2], northern_edge[2])
            height = height - acoustic_substep * ((zonal_wind_padded[:, 2:, 1:-1] - zonal_wind_padded[:, :-2, 1:-1]) + (meridional_wind_padded[:, 1:-1, 2:] - meridional_wind_padded[:, 1:-1, :-2]))
        qpad = framed_field(moist, western_edge[3], eastern_edge[3], southern_edge[3], northern_edge[3])
        flux = (jnp.maximum(uwind, 0.0) * (moist - qpad[:, :-2, 1:-1]) + jnp.minimum(uwind, 0.0) * (qpad[:, 2:, 1:-1] - moist)) + (jnp.maximum(meridional_wind, 0.0) * (moist - qpad[:, 1:-1, :-2]) + jnp.minimum(meridional_wind, 0.0) * (qpad[:, 1:-1, 2:] - moist))
        moist = moist - drift_step * flux
        excess = jnp.maximum(moist - saturation[:, None, None], 0.0)
        fallen = cond_rate[:, None, None] * excess
        moist = moist - fallen
        rain = rain + jnp.sum(fallen, axis=0)
    return height, uwind, meridional_wind, moist, rain


def reference(height, wind, moisture, coeffs, damping, vmix, basis, edge_source, row_cell, col_cell, cond_rate, saturation, ancestry):
    coeff_new = jnp.einsum('lj,mfjk->mflk', vmix, coeffs, precision=lax.Precision.HIGHEST) * damping
    coeff_low = coeff_new.astype(jnp.bfloat16).reshape(MEMBERS * 4 * LEV, KSPEC)
    rim = jnp.dot(coeff_low, basis, preferred_element_type=jnp.float32).reshape(MEMBERS, 4, LEV, RIM_G)
    west_all = jnp.take(rim, edge_source[:NY], axis=3)
    east_all = jnp.take(rim, edge_source[NY:2 * NY], axis=3)
    south_all = jnp.take(rim, edge_source[2 * NY:2 * NY + NX], axis=3)
    north_all = jnp.take(rim, edge_source[2 * NY + NX:], axis=3)
    row_table = (row_cell[None, :] == jnp.arange(GRX, dtype=jnp.int32)[:, None]).astype(jnp.float32)
    col_table = (col_cell[None, :] == jnp.arange(GRY, dtype=jnp.int32)[:, None]).astype(jnp.float32)
    row_count = jnp.sum(row_table, axis=1)
    col_count = jnp.sum(col_table, axis=1)
    heights, winds, moists, rains, coarses = [], [], [], [], []
    for member in range(MEMBERS):
        h_new, u_new, v_new, q_new, rain = member_run(height[member], wind[member, 0], wind[member, 1], moisture[member], west_all[member], east_all[member], south_all[member], north_all[member], cond_rate, saturation)
        partial_value = jnp.einsum('ax,lxy->lay', row_table, q_new, precision=lax.Precision.HIGHEST)
        sums = jnp.einsum('lay,by->lab', partial_value, col_table, precision=lax.Precision.HIGHEST)
        coarses.append(sums / (row_count[:, None] * col_count[None, :]))
        heights.append(h_new)
        winds.append(jnp.stack([u_new, v_new]))
        moists.append(q_new)
        rains.append(rain)
    height_all = jnp.stack(heights)
    wind_all = jnp.stack(winds)
    moist_all = jnp.stack(moists)
    rain_all = jnp.stack(rains)
    coarse_all = jnp.stack(coarses)
    return (jnp.take(height_all, ancestry, axis=0), jnp.take(wind_all, ancestry, axis=0), jnp.take(moist_all, ancestry, axis=0), jnp.take(rain_all, ancestry, axis=0), jnp.take(coarse_all, ancestry, axis=0), jnp.take(coeff_new, ancestry, axis=0))
```

```python
import functools

import jax
import jax.numpy as jnp
from jax import lax
from jax.experimental import pallas as pl
from jax.experimental.pallas import tpu as pltpu
from jax.sharding import PartitionSpec as P

RATIO = 8
ACOUSTIC = 2
HALO = 8
SPLIT = 3

acoustic_substep = 0.2
drift_step = 0.4

MESH = pl.DeviceIdType.MESH


def kernel(
    sizes,
    height,
    wind,
    moisture,
    coeffs_hbm,
    damping_hbm,
    vmix_hbm,
    basis_hbm,
    edge_source_hbm,
    row_cell_hbm,
    col_cell_hbm,
    cond_rate_hbm,
    saturation_hbm,
    ancestry_hbm,
    height_out,
    wind_out,
    moisture_out,
    rain_out,
    coarse_out,
    coeffs_out,
    coeffs,
    damping,
    vmix,
    basis,
    edge_source,
    row_cell,
    col_cell,
    cond_rate,
    saturation,
    ancestry,
    st,
    cf,
    st_sel,
    cf_sel,
    st_relay,
    cur,
    rows_out,
    rows_in,
    packed,
    packed_in,
    diag_in,
    rim_part,
    rim_in,
    rim_z,
    rim_full,
    table,
    sides,
    sides_t,
    coarse_rows_buf,
    coarse_part,
    coarse_in,
    halo_send,
    halo_recv,
    rim_send,
    rim_recv,
    rimz_send,
    rimz_recv,
    rimg_send,
    rimg_recv,
    crs_send,
    crs_recv,
    mem_send,
    mem_recv,
    local,
):
    members, count_x, count_y = sizes
    plane = count_x * count_y
    levels = st.shape[1]
    size_x = st.shape[3]
    size_y = st.shape[4]
    full_x = row_cell.shape[1]
    full_y = col_cell.shape[1]
    rim_points = basis.shape[1]
    coarse_x = coarse_out.shape[2]
    coarse_y = coarse_out.shape[3]
    share = rim_part.shape[1]
    f32 = jnp.float32

    z = lax.axis_index("mem")
    ix = lax.axis_index("gx")
    iy = lax.axis_index("gy")
    here = ix * count_y + iy
    low_side = z < 2
    inner = jnp.logical_and(z > 0, z < members - 1)
    outer = jnp.logical_not(inner)
    near = jnp.where(low_side, 1 - z, 5 - z)
    cross_inner = jnp.where(low_side, 2, 1)
    cross_outer = jnp.where(low_side, 3, 0)

    def plane_peer(step):
        other = lax.rem(here + step, plane)
        return other, other // count_y, lax.rem(other, count_y)

    loads = [
        (coeffs_hbm, coeffs),
        (damping_hbm, damping),
        (vmix_hbm, vmix),
        (height.at[0], st.at[z, :, 0]),
        (wind.at[0, 0], st.at[z, :, 1]),
        (wind.at[0, 1], st.at[z, :, 2]),
        (moisture.at[0], st.at[z, :, 3]),
        (basis_hbm, basis),
        (edge_source_hbm, edge_source),
        (row_cell_hbm, row_cell),
        (col_cell_hbm, col_cell),
        (cond_rate_hbm, cond_rate),
        (saturation_hbm, saturation),
        (ancestry_hbm, ancestry),
    ]
    copies = [pltpu.make_async_copy(a, b, local.at[n]) for n, (a, b) in enumerate(loads)]
    for copy in copies:
        copy.start()

    def ready(*which):
        for n in which:
            copies[n].wait()

    barrier = pltpu.get_barrier_semaphore()
    for step in range(1, plane):
        _, px, py = plane_peer(step)
        pl.semaphore_signal(barrier, inc=1, device_id=(z, px, py), device_id_type=MESH)
    for step in range(1, members):
        pl.semaphore_signal(
            barrier,
            inc=1,
            device_id=(lax.rem(z + step, members), ix, iy),
            device_id_type=MESH,
        )

    ready(0, 1, 2)
    new_fields = []
    for f in range(4):
        c = coeffs[0, f]
        acc = vmix[:, 0:1] * c[0:1]
        for j in range(1, levels):
            acc = acc + vmix[:, j : j + 1] * c[j : j + 1]
        new_fields.append(acc * damping[...])
    for f in range(4):
        cf[z, f // 2, f % 2] = new_fields[f]
    ready(3, 4, 5, 6)

    pl.semaphore_wait(barrier, plane - 1 + members - 1)

    def chunk(c, slot):
        return st.at[slot, c] if c < levels else cf.at[slot, c - levels]

    def chosen(c, way):
        return st_sel.at[way, c] if c < levels else cf_sel.at[way, c - levels]

    def z_copy(c, kind, src, slot, target, way):
        return pltpu.make_async_remote_copy(
            src_ref=src,
            dst_ref=chunk(c, slot),
            send_sem=mem_send.at[c, way],
            recv_sem=mem_recv.at[c, kind],
            device_id=(target, ix, iy),
            device_id_type=MESH,
        )

    def own_near(c):
        return z_copy(c, 0, chunk(c, z), z, near, 0)

    def own_cross(c):
        return z_copy(c, jnp.where(outer, 2, 1), chunk(c, z), z, cross_inner, 1)

    def sel_inner(c):
        return z_copy(c, 1, chosen(c, 0), z, cross_inner, 1)

    def sel_outer(c):
        return z_copy(c, 1, chosen(c, 1), z, cross_outer, 2)

    def relay_near(c):
        return z_copy(c, 0, st_relay, z, near, 0)

    def arrived(c, kind, slot):
        z_copy(c, kind, chunk(c, slot), slot, near, 0).wait_recv()

    first, rest = 0, list(range(1, levels))
    specs = [levels, levels + 1]

    @pl.when(inner)
    def _():
        own_cross(first).start()
        for c in rest:
            own_near(c).start()

    @pl.when(outer)
    def _():
        own_near(rest[0]).start()
        own_cross(first).start()
        for c in rest[1:] + [first] + specs:
            own_near(c).start()

    low = jnp.concatenate(new_fields, axis=0).astype(jnp.bfloat16)
    ready(7)
    part = jnp.dot(low, basis[...], preferred_element_type=f32)
    for g in range(count_x):
        rim_part[g] = part[g * share : (g + 1) * share]

    def rim_copy(step):
        _, px, py = plane_peer(step)
        return pltpu.make_async_remote_copy(
            src_ref=rim_part.at[px],
            dst_ref=rim_in.at[here],
            send_sem=rim_send.at[step],
            recv_sem=rim_recv.at[here],
            device_id=(z, px, py),
            device_id_type=MESH,
        )

    for step in range(1, plane):
        rim_copy(step).start()

    ready(8, 9, 10, 11, 12, 13)
    mine = ancestry[z]

    def select_near(c):
        arrived(c, 0, near)
        for way, target in ((0, cross_inner), (1, cross_outer)):
            take_own = ancestry[target] != near
            chosen(c, way)[...] = jnp.where(take_own, chunk(c, z)[...], chunk(c, near)[...])

    @pl.when(inner)
    def _():
        c = rest[0]
        select_near(c)
        sel_outer(c).start()
        sel_inner(c).start()

    n_edge = edge_source.shape[0]
    table[...] = (
        (lax.broadcasted_iota(jnp.int32, (rim_points, n_edge), 0)
         == edge_source[...].reshape(1, n_edge))
        .astype(f32)
        .astype(jnp.bfloat16)
    )
    row_table = (
        lax.broadcasted_iota(jnp.int32, (coarse_x, full_x), 0) == row_cell[...]
    ).astype(f32)
    row_count = jnp.sum(row_table, axis=1, keepdims=True)
    wide = lax.rem(
        lax.broadcasted_iota(jnp.int32, (levels * coarse_y, full_y), 0), coarse_y
    )
    col_table = (wide == col_cell[...]).astype(f32)
    col_count = lax.dot_general(
        jnp.ones((8, full_y), f32),
        col_table,
        (((1,), (1,)), ((), ())),
        preferred_element_type=f32,
    )[0:1]
    col_off = pl.multiple_of(iy * size_y, 128)
    row_off = pl.multiple_of(ix * size_x, 8)
    cells_here = col_cell[:, pl.ds(col_off, size_y)]
    wide_here = lax.broadcasted_iota(jnp.int32, (levels * coarse_y, size_y), 0)
    coarse_rows_buf[...] = jnp.zeros_like(coarse_rows_buf)

    total = rim_part[ix]
    for step in range(1, plane):
        other, px, py = plane_peer(step)
        pltpu.make_async_remote_copy(
            src_ref=rim_part.at[px],
            dst_ref=rim_in.at[other],
            send_sem=rim_send.at[step],
            recv_sem=rim_recv.at[other],
            device_id=(z, px, py),
            device_id_type=MESH,
        ).wait_recv()
        total = total + rim_in[other]
    rim_z[z] = total

    def rimz_copy(step, source):
        return pltpu.make_async_remote_copy(
            src_ref=rim_z.at[source],
            dst_ref=rim_z.at[source],
            send_sem=rimz_send.at[step],
            recv_sem=rimz_recv.at[source],
            device_id=(lax.rem(z + step, members), ix, iy),
            device_id_type=MESH,
        )

    for step in range(1, members):
        rimz_copy(step, z).start()

    @pl.when(inner)
    def _():
        arrived(first, 1, cross_inner)
        arrived(first, 2, cross_outer)
        want = ancestry[near]
        a = st[z, first]
        a = jnp.where(want == cross_inner, st[cross_inner, first], a)
        st_relay[...] = jnp.where(want == cross_outer, st[cross_outer, first], a)
        relay_near(first).start()
        for c in specs:
            own_near(c).start()
        for c in rest[1:]:
            select_near(c)
            sel_outer(c).start()
        for c in rest[1:]:
            sel_inner(c).start()

    share_sel = rim_z[z]
    for step in range(1, members):
        source = lax.rem(z + step, members)
        rimz_copy(step, source).wait_recv()
        share_sel = jnp.where(mine == source, rim_z[source], share_sel)
    rim_full[ix] = share_sel

    def rimg_copy(step, source):
        return pltpu.make_async_remote_copy(
            src_ref=rim_full.at[source],
            dst_ref=rim_full.at[source],
            send_sem=rimg_send.at[step],
            recv_sem=rimg_recv.at[source],
            device_id=(z, lax.rem(ix + step, count_x), iy),
            device_id_type=MESH,
        )

    for step in range(1, count_x):
        rimg_copy(step, ix).start()

    lane = lax.broadcasted_iota(jnp.int32, (size_x, size_y), 1)
    width = size_y // (4 * levels)
    half = width // 2

    def settle(c, ref):
        arrived(c, 1, cross_inner)

        @pl.when(outer)
        def _():
            arrived(c, 0, near)

        a = jnp.where(mine == z, chunk(c, z)[...], chunk(c, cross_inner)[...])
        ref[...] = jnp.where(mine == near, chunk(c, near)[...], a)

    @pl.when(outer)
    def _():
        arrived(first, 0, near)
        cur[first] = jnp.where(mine == z, st[z, first], st[near, first])

    @pl.when(inner)
    def _():
        arrived(first, 0, near)
        a = jnp.where(mine == cross_inner, st[cross_inner, first], st[cross_outer, first])
        a = jnp.where(mine == near, st[near, first], a)
        cur[first] = jnp.where(mine == z, st[z, first], a)
        for c in specs:
            select_near(c)
            sel_outer(c).start()
        for c in specs:
            sel_inner(c).start()

    groups = [list(range(SPLIT)), list(range(SPLIT, levels))]

    def halo_jobs(g, mode):
        lo, n_lev = groups[g][0], len(groups[g])
        lev = pl.ds(lo, n_lev)
        for dx in (-1, 0, 1):
            for dy in (-1, 0, 1):
                if dx == 0 and dy == 0:
                    continue
                flip = -1 if mode == "recv" else 1
                ok = jnp.bool_(True)
                if dx * flip == -1:
                    ok = jnp.logical_and(ok, ix > 0)
                if dx * flip == 1:
                    ok = jnp.logical_and(ok, ix < count_x - 1)
                if dy * flip == -1:
                    ok = jnp.logical_and(ok, iy > 0)
                if dy * flip == 1:
                    ok = jnp.logical_and(ok, iy < count_y - 1)
                sx = 0 if dx == -1 else 1
                sy = 0 if dy == -1 else 1
                rows = pl.ds(0, HALO) if dx == -1 else pl.ds(size_x - HALO, HALO)
                if dy == 0:
                    src, dst, base = rows_out.at[sx, lev], rows_in.at[sx, lev], sx
                elif dx == 0:
                    src, dst, base = packed.at[g], packed_in.at[g, sy], 2 + sy
                else:
                    src, dst = packed.at[g, rows, :], diag_in.at[g, sx, sy]
                    base = 4 + 2 * sx + sy

                def go(src=src, dst=dst, base=base, target=(z, ix + dx, iy + dy)):
                    copy = pltpu.make_async_remote_copy(
                        src_ref=src,
                        dst_ref=dst,
                        send_sem=halo_send.at[g, base],
                        recv_sem=halo_recv.at[g, base],
                        device_id=target,
                        device_id_type=MESH,
                    )
                    if mode == "start":
                        copy.start()
                    elif mode == "send":
                        copy.wait_send()
                    else:
                        copy.wait_recv()

                pl.when(ok)(go)

    def halo_out(g):
        pack = jnp.zeros((size_x, size_y), f32)
        for l in groups[g]:
            if l != first:
                settle(l, cur.at[l])
            for f in range(4):
                rows_out[0, l, f] = cur[l, f, 0:HALO]
                rows_out[1, l, f] = cur[l, f, size_x - HALO :]
                k = f * levels + l
                moved = pltpu.roll(cur[l, f], (width * k + half) % size_y, 1)
                pack = jnp.where(lane // width == k, moved, pack)
        packed[g] = pack
        halo_jobs(g, "start")

    halo_out(0)
    halo_out(1)

    ext_x = size_x + 2 * HALO
    ext_y = 2 * size_y
    rpos = lax.broadcasted_iota(jnp.int32, (ext_x, ext_y), 0)
    cpos = lax.broadcasted_iota(jnp.int32, (ext_x, ext_y), 1)
    gx_pos = ix * size_x + jnp.where(rpos < size_x + HALO, rpos, rpos - ext_x)
    gy_pos = iy * size_y + jnp.where(cpos < size_y + size_y // 2, cpos, cpos - ext_y)
    inside = (gx_pos >= 0) & (gx_pos < full_x) & (gy_pos >= 0) & (gy_pos < full_y)
    at_west = gx_pos == -1
    at_east = gx_pos == full_x
    at_south = gy_pos == -1

    for step in range(1, count_x):
        rimg_copy(step, lax.rem(ix + step, count_x)).wait_recv()
    rim = jnp.concatenate([rim_full[g] for g in range(count_x)], axis=0)
    rim_hi = rim.astype(jnp.bfloat16)
    rim_lo = (rim - rim_hi.astype(f32)).astype(jnp.bfloat16)
    both = jnp.dot(
        jnp.concatenate([rim_hi, rim_lo], axis=0), table[...], preferred_element_type=f32
    )
    n_rows = 4 * levels
    edge = both[0:n_rows] + both[n_rows:]
    sides[...] = edge
    for s in range(2):
        begin = 2 * full_y + s * full_x
        sides_t[s, HALO : HALO + full_x, :] = edge[:, begin : begin + full_x].T
        sides_t[s, 0:HALO, :] = jnp.zeros((HALO, n_rows), f32)
        sides_t[s, HALO + full_x :, :] = jnp.zeros((HALO, n_rows), f32)
    lane1 = lax.broadcasted_iota(jnp.int32, (n_rows, size_y), 1)

    def x_side(begin):
        own = sides[:, pl.ds(pl.multiple_of(begin + col_off, 128), size_y)]
        after = lax.rem(iy + 1, count_y) * size_y
        before = lax.rem(iy + count_y - 1, count_y) * size_y
        nxt_b = sides[:, pl.ds(pl.multiple_of(begin + after, 128), size_y)]
        prv_b = sides[:, pl.ds(pl.multiple_of(begin + before, 128), size_y)]
        return jnp.concatenate([own, jnp.where(lane1 < size_y // 2, nxt_b, prv_b)], axis=1)

    def y_side(s):
        body_rows = sides_t[s, pl.ds(pl.multiple_of(row_off + HALO, 8), size_x), :]
        above = sides_t[s, pl.ds(pl.multiple_of(row_off + HALO + size_x, 8), HALO), :]
        below = sides_t[s, pl.ds(row_off, HALO), :]
        return jnp.concatenate([body_rows, above, below], axis=0)

    west, east = x_side(0), x_side(full_y)
    south, north = y_side(0), y_side(1)

    lane2 = lax.broadcasted_iota(jnp.int32, (size_x + 2 * HALO, size_y), 1)
    take_next = lax.rem(lane2, width) >= half
    rain = jnp.zeros((size_x, size_y), f32)
    for l in range(levels):
        g = 0 if l < SPLIT else 1
        if l == groups[g][0]:
            halo_jobs(g, "recv")
            nxt = jnp.concatenate([packed_in[g, 0], diag_in[g, 0, 0], diag_in[g, 1, 0]], axis=0)
            prv = jnp.concatenate([packed_in[g, 1], diag_in[g, 0, 1], diag_in[g, 1, 1]], axis=0)
            mixed = jnp.where(take_next, nxt, prv)

        def extended(f):
            k = f * levels + l
            left = jnp.concatenate([cur[l, f], rows_in[0, l, f], rows_in[1, l, f]], axis=0)
            right = pltpu.roll(mixed, (size_y - (width * k + half)) % size_y, 1)
            return jnp.concatenate([left, right], axis=1)

        def outside(f):
            k = f * levels + l
            value = jnp.where(at_south, south[:, k : k + 1], north[:, k : k + 1])
            value = jnp.where(at_east, east[k : k + 1], value)
            return jnp.where(at_west, west[k : k + 1], value)

        def up(a):
            return pltpu.roll(a, ext_x - 1, 0)

        def down(a):
            return pltpu.roll(a, 1, 0)

        def right_of(a):
            return pltpu.roll(a, ext_y - 1, 1)

        def left_of(a):
            return pltpu.roll(a, 1, 1)

        bh, bu, bv, bq = outside(0), outside(1), outside(2), outside(3)
        h, u, v, q = extended(0), extended(1), extended(2), extended(3)
        h = jnp.where(inside, h, bh)
        q = jnp.where(inside, q, bq)
        for substep in range(ACOUSTIC):
            u = u - acoustic_substep * (up(h) - down(h))
            v = v - acoustic_substep * (right_of(h) - left_of(h))
            u = jnp.where(inside, u, bu)
            v = jnp.where(inside, v, bv)
            h = h - acoustic_substep * ((up(u) - down(u)) + (right_of(v) - left_of(v)))
            h = jnp.where(inside, h, bh)
        flux = (
            jnp.maximum(u, 0.0) * (q - down(q)) + jnp.minimum(u, 0.0) * (up(q) - q)
        ) + (
            jnp.maximum(v, 0.0) * (q - left_of(q)) + jnp.minimum(v, 0.0) * (right_of(q) - q)
        )
        q = (q - drift_step * flux)[0:size_x, 0:size_y]
        fallen = cond_rate[l] * jnp.maximum(q - saturation[l], 0.0)
        q_new = q - fallen
        height_out[0, l] = h[0:size_x, 0:size_y]
        wind_out[0, 0, l] = u[0:size_x, 0:size_y]
        wind_out[0, 1, l] = v[0:size_x, 0:size_y]
        moisture_out[0, l] = q_new
        rain = rain + fallen
        spread = ((wide_here - l * coarse_y) == cells_here).astype(f32)
        summed = lax.dot_general(
            q_new,
            spread,
            (((1,), (1,)), ((), ())),
            precision=lax.Precision.HIGHEST,
            preferred_element_type=f32,
        )
        rows_here = pl.ds(row_off, size_x)
        coarse_rows_buf[rows_here, :] = coarse_rows_buf[rows_here, :] + summed

    coarse_part[...] = jnp.dot(
        row_table,
        coarse_rows_buf[...],
        precision=lax.Precision.HIGHEST,
        preferred_element_type=f32,
    )

    def crs_copy(step, source):
        _, px, py = plane_peer(step)
        return pltpu.make_async_remote_copy(
            src_ref=coarse_part,
            dst_ref=coarse_in.at[source],
            send_sem=crs_send.at[step],
            recv_sem=crs_recv.at[source],
            device_id=(z, px, py),
            device_id_type=MESH,
        )

    for step in range(1, plane):
        crs_copy(step, here).start()
    rain_out[0] = rain

    for half_at, c in enumerate(specs):
        settle(c, coeffs_out.at[0, pl.ds(2 * half_at, 2)])

    total = coarse_part[...]
    for step in range(1, plane):
        other, _, _ = plane_peer(step)
        crs_copy(step, other).wait_recv()
        total = total + coarse_in[other]
    total = total / (row_count * col_count)
    for l in range(levels):
        coarse_out[0, l] = total[:, l * coarse_y : (l + 1) * coarse_y]

    for g in range(2):
        halo_jobs(g, "send")
    for step in range(1, plane):
        rim_copy(step).wait_send()
        crs_copy(step, here).wait_send()
    for step in range(1, count_x):
        rimg_copy(step, ix).wait_send()
    for step in range(1, members):
        rimz_copy(step, z).wait_send()
    for c in rest + specs:
        own_near(c).wait_send()
    own_cross(first).wait_send()

    @pl.when(outer)
    def _():
        own_near(first).wait_send()

    @pl.when(inner)
    def _():
        relay_near(first).wait_send()
        for c in rest + specs:
            sel_inner(c).wait_send()
            sel_outer(c).wait_send()


def write_out(*refs):
    sems = refs[12]
    copies = [pltpu.make_async_copy(refs[n], refs[6 + n], sems.at[n]) for n in range(6)]
    for copy in copies:
        copy.start()
    for copy in copies:
        copy.wait()


def body(
    sizes,
    height,
    wind,
    moisture,
    coeffs,
    damping,
    vmix,
    basis,
    edge_source,
    row_cell,
    col_cell,
    cond_rate,
    saturation,
    ancestry,
):
    members, count_x, count_y = sizes
    plane = count_x * count_y
    _, levels, size_x, size_y = height.shape
    local_k = coeffs.shape[3]
    rim_points = basis.shape[1]
    full_x = row_cell.shape[0]
    full_y = col_cell.shape[0]
    n_edge = edge_source.shape[0]
    coarse_x, coarse_y = full_x // RATIO, full_y // RATIO
    share = 4 * levels // count_x
    rows = 4 * levels
    f32 = jnp.float32
    vmem = pl.BlockSpec(memory_space=pltpu.VMEM)
    dma = pltpu.SemaphoreType.DMA
    coarse_chunk = (coarse_x, levels * coarse_y)
    operands = (
        height,
        wind,
        moisture,
        coeffs,
        damping.reshape(1, -1),
        vmix,
        basis,
        edge_source,
        row_cell.reshape(1, -1),
        col_cell.reshape(1, -1),
        cond_rate,
        saturation,
        ancestry,
    )
    chunks = levels + 2
    scratch = [
        *[pltpu.VMEM(a.shape, a.dtype) for a in operands[3:10]],
        *[pltpu.SMEM(a.shape, a.dtype) for a in operands[10:]],
        pltpu.VMEM((members, levels, 4, size_x, size_y), f32),
        pltpu.VMEM((members, 2, 2, levels, local_k), f32),
        pltpu.VMEM((2, levels, 4, size_x, size_y), f32),
        pltpu.VMEM((2, 2, 2, levels, local_k), f32),
        pltpu.VMEM((4, size_x, size_y), f32),
        pltpu.VMEM((levels, 4, size_x, size_y), f32),
        pltpu.VMEM((2, levels, 4, HALO, size_y), f32),
        pltpu.VMEM((2, levels, 4, HALO, size_y), f32),
        pltpu.VMEM((2, size_x, size_y), f32),
        pltpu.VMEM((2, 2, size_x, size_y), f32),
        pltpu.VMEM((2, 2, 2, HALO, size_y), f32),
        pltpu.VMEM((count_x, share, rim_points), f32),
        pltpu.VMEM((plane, share, rim_points), f32),
        pltpu.VMEM((members, share, rim_points), f32),
        pltpu.VMEM((count_x, share, rim_points), f32),
        pltpu.VMEM((rim_points, n_edge), jnp.bfloat16),
        pltpu.VMEM((rows, n_edge), f32),
        pltpu.VMEM((2, full_x + 2 * HALO, rows), f32),
        pltpu.VMEM((full_x, levels * coarse_y), f32),
        pltpu.VMEM(coarse_chunk, f32),
        pltpu.VMEM((plane, *coarse_chunk), f32),
        dma((2, 8)),
        dma((2, 8)),
        dma((plane,)),
        dma((plane,)),
        dma((members,)),
        dma((members,)),
        dma((count_x,)),
        dma((count_x,)),
        dma((plane,)),
        dma((plane,)),
        dma((chunks, 3)),
        dma((chunks, 3)),
        dma((14,)),
    ]
    outs = (
        pltpu.VMEM(height.shape, f32),
        pltpu.VMEM(wind.shape, f32),
        pltpu.VMEM(moisture.shape, f32),
        pltpu.VMEM((1, size_x, size_y), f32),
        pltpu.VMEM((1, levels, coarse_x, coarse_y), f32),
        pltpu.VMEM(coeffs.shape, f32),
    )
    results = pl.pallas_call(
        functools.partial(kernel, sizes),
        out_shape=outs,
        in_specs=[pl.BlockSpec(memory_space=pltpu.HBM)] * 13,
        out_specs=(vmem,) * 6,
        scratch_shapes=scratch,
        compiler_params=pltpu.CompilerParams(
            collective_id=0, has_side_effects=True, vmem_limit_bytes=36 * 1024 * 1024
        ),
    )(*[pltpu.with_memory_space_constraint(a, pltpu.HBM) for a in operands])
    return pl.pallas_call(
        write_out,
        out_shape=tuple(jax.ShapeDtypeStruct(r.shape, f32) for r in results),
        in_specs=[vmem] * 6,
        out_specs=(pl.BlockSpec(memory_space=pl.ANY),) * 6,
        scratch_shapes=[dma((6,))],
        compiler_params=pltpu.CompilerParams(vmem_limit_bytes=8 * 1024 * 1024),
    )(*results)


def solution(mesh):
    sizes = (mesh.shape["mem"], mesh.shape["gx"], mesh.shape["gy"])
    in_specs = (
        P("mem", None, "gx", "gy"),
        P("mem", None, None, "gx", "gy"),
        P("mem", None, "gx", "gy"),
        P("mem", None, None, ("gx", "gy")),
        P(("gx", "gy")),
        P(),
        P(("gx", "gy"), None),
        P(),
        P(),
        P(),
        P(),
        P(),
        P(),
    )
    out_specs = (
        P("mem", None, "gx", "gy"),
        P("mem", None, None, "gx", "gy"),
        P("mem", None, "gx", "gy"),
        P("mem", "gx", "gy"),
        P("mem", None, None, None),
        P("mem", None, None, ("gx", "gy")),
    )
    return jax.shard_map(
        functools.partial(body, sizes),
        mesh=mesh,
        in_specs=in_specs,
        out_specs=out_specs,
        check_vma=False,
    )
```

```python
import functools

import jax
import jax.numpy as jnp
from jax import lax
from jax.experimental import pallas as pl
from jax.experimental.pallas import tpu as pltpu
from jax.sharding import PartitionSpec as P

RATIO = 8
ACOUSTIC = 2
HALO = 8
SPLIT = 3

acoustic_substep = 0.2
drift_step = 0.4

MESH = pl.DeviceIdType.MESH


def kernel(
    sizes,
    height,
    wind,
    moisture,
    coeffs_hbm,
    damping_hbm,
    vmix_hbm,
    basis_hbm,
    edge_source_hbm,
    row_cell_hbm,
    col_cell_hbm,
    cond_rate_hbm,
    saturation_hbm,
    ancestry_hbm,
    height_out,
    wind_out,
    moisture_out,
    rain_out,
    coarse_out,
    coeffs_out,
    coeffs,
    damping,
    vmix,
    basis,
    edge_source,
    row_cell,
    col_cell,
    cond_rate,
    saturation,
    ancestry,
    st,
    cf,
    st_sel,
    cf_sel,
    st_relay,
    cur,
    rows_out,
    rows_in,
    packed,
    packed_in,
    diag_in,
    rim_part,
    rim_in,
    rim_z,
    rim_full,
    table,
    sides,
    sides_t,
    coarse_rows_buf,
    coarse_part,
    coarse_in,
    halo_recv,
    batch,
    mem_send,
    mem_recv,
    local,
):
    members, count_x, count_y = sizes
    plane = count_x * count_y
    levels = cur.shape[0]
    size_x = st.shape[2]
    size_y = st.shape[3]
    full_x = row_cell.shape[1]
    full_y = col_cell.shape[1]
    rim_points = basis.shape[1]
    coarse_x = coarse_out.shape[2]
    coarse_y = coarse_out.shape[3]
    share = rim_part.shape[1]
    f32 = jnp.float32

    z = lax.axis_index("mem")
    ix = lax.axis_index("gx")
    iy = lax.axis_index("gy")
    here = ix * count_y + iy
    low_side = z < 2
    inner = jnp.logical_and(z > 0, z < members - 1)
    outer = jnp.logical_not(inner)
    near = jnp.where(low_side, 1 - z, 5 - z)
    cross_inner = jnp.where(low_side, 2, 1)
    cross_outer = jnp.where(low_side, 3, 0)

    def plane_peer(step):
        other = lax.rem(here + step, plane)
        return other, other // count_y, lax.rem(other, count_y)

    own_slots = pl.ds(z * levels, levels)
    loads = [
        (coeffs_hbm, coeffs),
        (damping_hbm, damping),
        (vmix_hbm, vmix),
        (height.at[0], st.at[own_slots, 0]),
        (wind.at[0, 0], st.at[own_slots, 1]),
        (wind.at[0, 1], st.at[own_slots, 2]),
        (moisture.at[0], st.at[own_slots, 3]),
        (basis_hbm, basis),
        (edge_source_hbm, edge_source),
        (row_cell_hbm, row_cell),
        (col_cell_hbm, col_cell),
        (cond_rate_hbm, cond_rate),
        (saturation_hbm, saturation),
        (ancestry_hbm, ancestry),
    ]
    copies = [pltpu.make_async_copy(a, b, local.at[n]) for n, (a, b) in enumerate(loads)]
    for copy in copies:
        copy.start()

    def ready(*which):
        for n in which:
            copies[n].wait()

    barrier = pltpu.get_barrier_semaphore()
    for step in range(1, plane):
        _, px, py = plane_peer(step)
        pl.semaphore_signal(barrier, inc=1, device_id=(z, px, py), device_id_type=MESH)
    for step in range(1, members):
        pl.semaphore_signal(
            barrier,
            inc=1,
            device_id=(lax.rem(z + step, members), ix, iy),
            device_id_type=MESH,
        )

    ready(0, 1, 2)
    new_fields = []
    for f in range(4):
        c = coeffs[0, f]
        acc = vmix[:, 0:1] * c[0:1]
        for j in range(1, levels):
            acc = acc + vmix[:, j : j + 1] * c[j : j + 1]
        new_fields.append(acc * damping[...])
    for f in range(4):
        cf[2 * z + f // 2, f % 2] = new_fields[f]
    ready(3, 4, 5, 6)

    pl.semaphore_wait(barrier, plane - 1 + members - 1)

    def chunk(c, slot):
        return st.at[slot * levels + c] if c < levels else cf.at[slot * 2 + c - levels]

    def chosen(c, way):
        return st_sel.at[way, c] if c < levels else cf_sel.at[way, c - levels]

    def z_copy(c, kind, src, slot, target):
        return pltpu.make_async_remote_copy(
            src_ref=src,
            dst_ref=chunk(c, slot),
            send_sem=mem_send.at[0 if c < levels else 1],
            recv_sem=mem_recv.at[kind if c == 0 else 1 + 2 * c + kind],
            device_id=(target, ix, iy),
            device_id_type=MESH,
        )

    def own_near(c):
        return z_copy(c, 0, chunk(c, z), z, near)

    def own_cross(c):
        return z_copy(c, jnp.where(outer, 2, 1), chunk(c, z), z, cross_inner)

    def sel_inner(c):
        return z_copy(c, 1, chosen(c, 0), z, cross_inner)

    def sel_outer(c):
        return z_copy(c, 1, chosen(c, 1), z, cross_outer)

    def relay_near(c):
        return z_copy(c, 0, st_relay, z, near)

    def arrived(c, kind, slot):
        z_copy(c, kind, chunk(c, slot), slot, near).wait_recv()

    first, rest = 0, list(range(1, levels))
    specs = [levels, levels + 1]

    @pl.when(inner)
    def _():
        own_cross(first).start()
        for c in rest:
            own_near(c).start()

    @pl.when(outer)
    def _():
        own_near(rest[0]).start()
        own_cross(first).start()
        own_near(rest[1]).start()

    low = jnp.concatenate(new_fields, axis=0).astype(jnp.bfloat16)
    ready(7)
    part = jnp.dot(low, basis[...], preferred_element_type=f32)
    for g in range(count_x):
        rim_part[g] = part[g * share : (g + 1) * share]

    def rim_copy(step):
        _, px, py = plane_peer(step)
        return pltpu.make_async_remote_copy(
            src_ref=rim_part.at[px],
            dst_ref=rim_in.at[here],
            send_sem=batch.at[0],
            recv_sem=batch.at[1],
            device_id=(z, px, py),
            device_id_type=MESH,
        )

    for step in range(1, plane):
        rim_copy(step).start()

    ready(8, 9, 10, 11, 12, 13)
    mine = ancestry[z]

    def select_near(c):
        arrived(c, 0, near)
        for way, target in ((0, cross_inner), (1, cross_outer)):
            take_own = ancestry[target] != near
            chosen(c, way)[...] = jnp.where(take_own, chunk(c, z)[...], chunk(c, near)[...])

    n_edge = edge_source.shape[0]
    table[...] = (
        (lax.broadcasted_iota(jnp.int32, (rim_points, n_edge), 0)
         == edge_source[...].reshape(1, n_edge))
        .astype(f32)
        .astype(jnp.bfloat16)
    )
    row_table = (
        lax.broadcasted_iota(jnp.int32, (coarse_x, full_x), 0) == row_cell[...]
    ).astype(f32)
    row_count = jnp.sum(row_table, axis=1, keepdims=True)
    wide = lax.rem(
        lax.broadcasted_iota(jnp.int32, (levels * coarse_y, full_y), 0), coarse_y
    )
    col_table = (wide == col_cell[...]).astype(f32)
    col_count = lax.dot_general(
        jnp.ones((8, full_y), f32),
        col_table,
        (((1,), (1,)), ((), ())),
        preferred_element_type=f32,
    )[0:1]
    col_off = pl.multiple_of(iy * size_y, 128)
    row_off = pl.multiple_of(ix * size_x, 8)
    cells_here = col_cell[:, pl.ds(col_off, size_y)]
    wide_here = lax.broadcasted_iota(jnp.int32, (levels * coarse_y, size_y), 0)
    coarse_rows_buf[...] = jnp.zeros_like(coarse_rows_buf)

    def batch_of(n, ref, count):
        many = ref.at[pl.ds(0, count)]
        return pltpu.make_async_remote_copy(
            src_ref=many,
            dst_ref=many,
            send_sem=batch.at[n],
            recv_sem=batch.at[n + 1],
            device_id=(near, ix, iy),
            device_id_type=MESH,
        )

    batch_of(0, rim_in, plane - 1).wait_recv()
    total = rim_part[ix]
    for step in range(1, plane):
        other, _, _ = plane_peer(step)
        total = total + rim_in[other]
    rim_z[z] = total

    def rimz_copy(step, source):
        return pltpu.make_async_remote_copy(
            src_ref=rim_z.at[source],
            dst_ref=rim_z.at[source],
            send_sem=batch.at[2],
            recv_sem=batch.at[3],
            device_id=(lax.rem(z + step, members), ix, iy),
            device_id_type=MESH,
        )

    for step in range(1, members):
        rimz_copy(step, z).start()

    @pl.when(outer)
    def _():
        for c in rest[2:] + [first] + specs:
            own_near(c).start()

    @pl.when(inner)
    def _():
        select_near(rest[0])
        sel_outer(rest[0]).start()
        sel_inner(rest[0]).start()
        arrived(first, 1, cross_inner)
        arrived(first, 2, cross_outer)
        want = ancestry[near]
        a = chunk(first, z)[...]
        a = jnp.where(want == cross_inner, chunk(first, cross_inner)[...], a)
        st_relay[...] = jnp.where(want == cross_outer, chunk(first, cross_outer)[...], a)
        relay_near(first).start()
        for c in specs:
            own_near(c).start()
        for c in rest[1:]:
            select_near(c)
            sel_outer(c).start()
        for c in rest[1:]:
            sel_inner(c).start()

    batch_of(2, rim_z, members - 1).wait_recv()
    share_sel = rim_z[z]
    for step in range(1, members):
        source = lax.rem(z + step, members)
        share_sel = jnp.where(mine == source, rim_z[source], share_sel)
    rim_full[ix] = share_sel

    def rimg_copy(step, source):
        return pltpu.make_async_remote_copy(
            src_ref=rim_full.at[source],
            dst_ref=rim_full.at[source],
            send_sem=batch.at[4],
            recv_sem=batch.at[5],
            device_id=(z, lax.rem(ix + step, count_x), iy),
            device_id_type=MESH,
        )

    for step in range(1, count_x):
        rimg_copy(step, ix).start()

    lane = lax.broadcasted_iota(jnp.int32, (size_x, size_y), 1)
    width = size_y // (4 * levels)
    half = width // 2

    def settle(c, ref):
        arrived(c, 1, cross_inner)

        @pl.when(outer)
        def _():
            arrived(c, 0, near)

        a = jnp.where(mine == z, chunk(c, z)[...], chunk(c, cross_inner)[...])
        ref[...] = jnp.where(mine == near, chunk(c, near)[...], a)

    @pl.when(outer)
    def _():
        arrived(first, 0, near)
        cur[first] = jnp.where(mine == z, chunk(first, z)[...], chunk(first, near)[...])

    @pl.when(inner)
    def _():
        arrived(first, 0, near)
        a = chunk(first, cross_outer)[...]
        a = jnp.where(mine == cross_inner, chunk(first, cross_inner)[...], a)
        a = jnp.where(mine == near, chunk(first, near)[...], a)
        cur[first] = jnp.where(mine == z, chunk(first, z)[...], a)
        for c in specs:
            select_near(c)
            sel_outer(c).start()
        for c in specs:
            sel_inner(c).start()

    groups = [list(range(SPLIT)), list(range(SPLIT, levels))]

    def halo_jobs(g, mode):
        lo, n_lev = groups[g][0], len(groups[g])
        lev = pl.ds(lo, n_lev)
        for dx in (-1, 0, 1):
            for dy in (-1, 0, 1):
                if dx == 0 and dy == 0:
                    continue
                flip = -1 if mode == "recv" else 1
                ok = jnp.bool_(True)
                if dx * flip == -1:
                    ok = jnp.logical_and(ok, ix > 0)
                if dx * flip == 1:
                    ok = jnp.logical_and(ok, ix < count_x - 1)
                if dy * flip == -1:
                    ok = jnp.logical_and(ok, iy > 0)
                if dy * flip == 1:
                    ok = jnp.logical_and(ok, iy < count_y - 1)
                sx = 0 if dx == -1 else 1
                sy = 0 if dy == -1 else 1
                rows = pl.ds(0, HALO) if dx == -1 else pl.ds(size_x - HALO, HALO)
                if dy == 0:
                    src, dst, base = rows_out.at[sx, lev], rows_in.at[sx, lev], sx
                elif dx == 0:
                    src, dst, base = packed.at[g], packed_in.at[g, sy], 2 + sy
                else:
                    src, dst = packed.at[g, rows, :], diag_in.at[g, sx, sy]
                    base = 4 + 2 * sx + sy

                def go(src=src, dst=dst, base=base, target=(z, ix + dx, iy + dy)):
                    copy = pltpu.make_async_remote_copy(
                        src_ref=src,
                        dst_ref=dst,
                        send_sem=local.at[8 * g + base],
                        recv_sem=halo_recv.at[8 * g + base],
                        device_id=target,
                        device_id_type=MESH,
                    )
                    if mode == "start":
                        copy.start()
                    elif mode == "send":
                        copy.wait_send()
                    else:
                        copy.wait_recv()

                pl.when(ok)(go)

    def halo_out(g):
        pack = jnp.zeros((size_x, size_y), f32)
        for l in groups[g]:
            if l != first:
                settle(l, cur.at[l])
            for f in range(4):
                rows_out[0, l, f] = cur[l, f, 0:HALO]
                rows_out[1, l, f] = cur[l, f, size_x - HALO :]
                k = f * levels + l
                moved = pltpu.roll(cur[l, f], (width * k + half) % size_y, 1)
                pack = jnp.where(lane // width == k, moved, pack)
        packed[g] = pack
        halo_jobs(g, "start")

    halo_out(0)
    halo_out(1)

    ext_x = size_x + 2 * HALO
    ext_y = 2 * size_y
    rpos = lax.broadcasted_iota(jnp.int32, (ext_x, ext_y), 0)
    cpos = lax.broadcasted_iota(jnp.int32, (ext_x, ext_y), 1)
    gx_pos = ix * size_x + jnp.where(rpos < size_x + HALO, rpos, rpos - ext_x)
    gy_pos = iy * size_y + jnp.where(cpos < size_y + size_y // 2, cpos, cpos - ext_y)
    inside = (gx_pos >= 0) & (gx_pos < full_x) & (gy_pos >= 0) & (gy_pos < full_y)
    at_west = gx_pos == -1
    at_east = gx_pos == full_x
    at_south = gy_pos == -1

    batch_of(4, rim_full, count_x - 1).wait_recv()
    rim = jnp.concatenate([rim_full[g] for g in range(count_x)], axis=0)
    rim_hi = rim.astype(jnp.bfloat16)
    rim_lo = (rim - rim_hi.astype(f32)).astype(jnp.bfloat16)
    both = jnp.dot(
        jnp.concatenate([rim_hi, rim_lo], axis=0), table[...], preferred_element_type=f32
    )
    n_rows = 4 * levels
    edge = both[0:n_rows] + both[n_rows:]
    sides[...] = edge
    for s in range(2):
        begin = 2 * full_y + s * full_x
        sides_t[s, HALO : HALO + full_x, :] = edge[:, begin : begin + full_x].T
        sides_t[s, 0:HALO, :] = jnp.zeros((HALO, n_rows), f32)
        sides_t[s, HALO + full_x :, :] = jnp.zeros((HALO, n_rows), f32)
    lane1 = lax.broadcasted_iota(jnp.int32, (n_rows, size_y), 1)

    def x_side(begin):
        own = sides[:, pl.ds(pl.multiple_of(begin + col_off, 128), size_y)]
        after = lax.rem(iy + 1, count_y) * size_y
        before = lax.rem(iy + count_y - 1, count_y) * size_y
        nxt_b = sides[:, pl.ds(pl.multiple_of(begin + after, 128), size_y)]
        prv_b = sides[:, pl.ds(pl.multiple_of(begin + before, 128), size_y)]
        return jnp.concatenate([own, jnp.where(lane1 < size_y // 2, nxt_b, prv_b)], axis=1)

    def y_side(s):
        body_rows = sides_t[s, pl.ds(pl.multiple_of(row_off + HALO, 8), size_x), :]
        above = sides_t[s, pl.ds(pl.multiple_of(row_off + HALO + size_x, 8), HALO), :]
        below = sides_t[s, pl.ds(row_off, HALO), :]
        return jnp.concatenate([body_rows, above, below], axis=0)

    west, east = x_side(0), x_side(full_y)
    south, north = y_side(0), y_side(1)

    lane2 = lax.broadcasted_iota(jnp.int32, (size_x + 2 * HALO, size_y), 1)
    take_next = lax.rem(lane2, width) >= half
    rain = jnp.zeros((size_x, size_y), f32)
    for l in range(levels):
        g = 0 if l < SPLIT else 1
        if l == groups[g][0]:
            halo_jobs(g, "recv")
            nxt = jnp.concatenate([packed_in[g, 0], diag_in[g, 0, 0], diag_in[g, 1, 0]], axis=0)
            prv = jnp.concatenate([packed_in[g, 1], diag_in[g, 0, 1], diag_in[g, 1, 1]], axis=0)
            mixed = jnp.where(take_next, nxt, prv)

        def extended(f):
            k = f * levels + l
            left = jnp.concatenate([cur[l, f], rows_in[0, l, f], rows_in[1, l, f]], axis=0)
            right = pltpu.roll(mixed, (size_y - (width * k + half)) % size_y, 1)
            return jnp.concatenate([left, right], axis=1)

        def outside(f):
            k = f * levels + l
            value = jnp.where(at_south, south[:, k : k + 1], north[:, k : k + 1])
            value = jnp.where(at_east, east[k : k + 1], value)
            return jnp.where(at_west, west[k : k + 1], value)

        def up(a):
            return pltpu.roll(a, ext_x - 1, 0)

        def down(a):
            return pltpu.roll(a, 1, 0)

        def right_of(a):
            return pltpu.roll(a, ext_y - 1, 1)

        def left_of(a):
            return pltpu.roll(a, 1, 1)

        bh, bu, bv, bq = outside(0), outside(1), outside(2), outside(3)
        h, u, v, q = extended(0), extended(1), extended(2), extended(3)
        h = jnp.where(inside, h, bh)
        q = jnp.where(inside, q, bq)
        for substep in range(ACOUSTIC):
            u = u - acoustic_substep * (up(h) - down(h))
            v = v - acoustic_substep * (right_of(h) - left_of(h))
            u = jnp.where(inside, u, bu)
            v = jnp.where(inside, v, bv)
            h = h - acoustic_substep * ((up(u) - down(u)) + (right_of(v) - left_of(v)))
            h = jnp.where(inside, h, bh)
        flux = (
            jnp.maximum(u, 0.0) * (q - down(q)) + jnp.minimum(u, 0.0) * (up(q) - q)
        ) + (
            jnp.maximum(v, 0.0) * (q - left_of(q)) + jnp.minimum(v, 0.0) * (right_of(q) - q)
        )
        q = (q - drift_step * flux)[0:size_x, 0:size_y]
        fallen = cond_rate[l] * jnp.maximum(q - saturation[l], 0.0)
        q_new = q - fallen
        height_out[0, l] = h[0:size_x, 0:size_y]
        wind_out[0, 0, l] = u[0:size_x, 0:size_y]
        wind_out[0, 1, l] = v[0:size_x, 0:size_y]
        moisture_out[0, l] = q_new
        rain = rain + fallen
        spread = ((wide_here - l * coarse_y) == cells_here).astype(f32)
        summed = lax.dot_general(
            q_new,
            spread,
            (((1,), (1,)), ((), ())),
            precision=lax.Precision.HIGHEST,
            preferred_element_type=f32,
        )
        rows_here = pl.ds(row_off, size_x)
        coarse_rows_buf[rows_here, :] = coarse_rows_buf[rows_here, :] + summed

    coarse_part[...] = jnp.dot(
        row_table,
        coarse_rows_buf[...],
        precision=lax.Precision.HIGHEST,
        preferred_element_type=f32,
    )

    def crs_copy(step, source):
        _, px, py = plane_peer(step)
        return pltpu.make_async_remote_copy(
            src_ref=coarse_part,
            dst_ref=coarse_in.at[source],
            send_sem=batch.at[6],
            recv_sem=batch.at[7],
            device_id=(z, px, py),
            device_id_type=MESH,
        )

    for step in range(1, plane):
        crs_copy(step, here).start()
    rain_out[0] = rain

    for half_at, c in enumerate(specs):
        settle(c, coeffs_out.at[0, pl.ds(2 * half_at, 2)])

    batch_of(6, coarse_in, plane - 1).wait_recv()
    total = coarse_part[...]
    for step in range(1, plane):
        other, _, _ = plane_peer(step)
        total = total + coarse_in[other]
    total = total / (row_count * col_count)
    for l in range(levels):
        coarse_out[0, l] = total[:, l * coarse_y : (l + 1) * coarse_y]

    for g in range(2):
        halo_jobs(g, "send")
    batch_of(0, rim_in, plane - 1).wait_send()
    batch_of(2, rim_z, members - 1).wait_send()
    batch_of(4, rim_full, count_x - 1).wait_send()
    batch_of(6, coarse_in, plane - 1).wait_send()

    def sent(n, ref, count):
        many = ref.at[pl.ds(0, count)]
        pltpu.make_async_remote_copy(
            src_ref=many,
            dst_ref=many,
            send_sem=mem_send.at[n],
            recv_sem=mem_recv.at[0],
            device_id=(near, ix, iy),
            device_id_type=MESH,
        ).wait_send()

    @pl.when(outer)
    def _():
        sent(0, st, levels + 1)
        sent(1, cf, 2)

    @pl.when(inner)
    def _():
        sent(0, st, 3 * levels - 1)
        sent(1, cf, 6)


def write_out(*refs):
    sems = refs[12]
    copies = [pltpu.make_async_copy(refs[n], refs[6 + n], sems.at[n]) for n in range(6)]
    for copy in copies:
        copy.start()
    for copy in copies:
        copy.wait()


def body(
    sizes,
    height,
    wind,
    moisture,
    coeffs,
    damping,
    vmix,
    basis,
    edge_source,
    row_cell,
    col_cell,
    cond_rate,
    saturation,
    ancestry,
):
    members, count_x, count_y = sizes
    plane = count_x * count_y
    _, levels, size_x, size_y = height.shape
    local_k = coeffs.shape[3]
    rim_points = basis.shape[1]
    full_x = row_cell.shape[0]
    full_y = col_cell.shape[0]
    n_edge = edge_source.shape[0]
    coarse_x, coarse_y = full_x // RATIO, full_y // RATIO
    share = 4 * levels // count_x
    rows = 4 * levels
    f32 = jnp.float32
    vmem = pl.BlockSpec(memory_space=pltpu.VMEM)
    dma = pltpu.SemaphoreType.DMA
    coarse_chunk = (coarse_x, levels * coarse_y)
    operands = (
        height,
        wind,
        moisture,
        coeffs,
        damping.reshape(1, -1),
        vmix,
        basis,
        edge_source,
        row_cell.reshape(1, -1),
        col_cell.reshape(1, -1),
        cond_rate,
        saturation,
        ancestry,
    )
    chunks = levels + 2
    scratch = [
        *[pltpu.VMEM(a.shape, a.dtype) for a in operands[3:10]],
        *[pltpu.SMEM(a.shape, a.dtype) for a in operands[10:]],
        pltpu.VMEM((members * levels, 4, size_x, size_y), f32),
        pltpu.VMEM((members * 2, 2, levels, local_k), f32),
        pltpu.VMEM((2, levels, 4, size_x, size_y), f32),
        pltpu.VMEM((2, 2, 2, levels, local_k), f32),
        pltpu.VMEM((4, size_x, size_y), f32),
        pltpu.VMEM((levels, 4, size_x, size_y), f32),
        pltpu.VMEM((2, levels, 4, HALO, size_y), f32),
        pltpu.VMEM((2, levels, 4, HALO, size_y), f32),
        pltpu.VMEM((2, size_x, size_y), f32),
        pltpu.VMEM((2, 2, size_x, size_y), f32),
        pltpu.VMEM((2, 2, 2, HALO, size_y), f32),
        pltpu.VMEM((count_x, share, rim_points), f32),
        pltpu.VMEM((plane, share, rim_points), f32),
        pltpu.VMEM((members, share, rim_points), f32),
        pltpu.VMEM((count_x, share, rim_points), f32),
        pltpu.VMEM((rim_points, n_edge), jnp.bfloat16),
        pltpu.VMEM((rows, n_edge), f32),
        pltpu.VMEM((2, full_x + 2 * HALO, rows), f32),
        pltpu.VMEM((full_x, levels * coarse_y), f32),
        pltpu.VMEM(coarse_chunk, f32),
        pltpu.VMEM((plane, *coarse_chunk), f32),
        dma((16,)),
        dma((8,)),
        dma((2,)),
        dma((1 + 2 * chunks,)),
        dma((16,)),
    ]
    outs = (
        pltpu.VMEM(height.shape, f32),
        pltpu.VMEM(wind.shape, f32),
        pltpu.VMEM(moisture.shape, f32),
        pltpu.VMEM((1, size_x, size_y), f32),
        pltpu.VMEM((1, levels, coarse_x, coarse_y), f32),
        pltpu.VMEM(coeffs.shape, f32),
    )
    results = pl.pallas_call(
        functools.partial(kernel, sizes),
        out_shape=outs,
        in_specs=[pl.BlockSpec(memory_space=pltpu.HBM)] * 13,
        out_specs=(vmem,) * 6,
        scratch_shapes=scratch,
        compiler_params=pltpu.CompilerParams(
            collective_id=0, has_side_effects=True, vmem_limit_bytes=36 * 1024 * 1024
        ),
    )(*[pltpu.with_memory_space_constraint(a, pltpu.HBM) for a in operands])
    return pl.pallas_call(
        write_out,
        out_shape=tuple(jax.ShapeDtypeStruct(r.shape, f32) for r in results),
        in_specs=[vmem] * 6,
        out_specs=(pl.BlockSpec(memory_space=pl.ANY),) * 6,
        scratch_shapes=[dma((6,))],
        compiler_params=pltpu.CompilerParams(vmem_limit_bytes=8 * 1024 * 1024),
    )(*results)


def solution(mesh):
    sizes = (mesh.shape["mem"], mesh.shape["gx"], mesh.shape["gy"])
    in_specs = (
        P("mem", None, "gx", "gy"),
        P("mem", None, None, "gx", "gy"),
        P("mem", None, "gx", "gy"),
        P("mem", None, None, ("gx", "gy")),
        P(("gx", "gy")),
        P(),
        P(("gx", "gy"), None),
        P(),
        P(),
        P(),
        P(),
        P(),
        P(),
    )
    out_specs = (
        P("mem", None, "gx", "gy"),
        P("mem", None, None, "gx", "gy"),
        P("mem", None, "gx", "gy"),
        P("mem", "gx", "gy"),
        P("mem", None, None, None),
        P("mem", None, None, ("gx", "gy")),
    )
    return jax.shard_map(
        functools.partial(body, sizes),
        mesh=mesh,
        in_specs=in_specs,
        out_specs=out_specs,
        check_vma=False,
    )
```

```python
import functools

import jax
import jax.numpy as jnp
from jax import lax
from jax.experimental import pallas as pl
from jax.experimental.pallas import tpu as pltpu
from jax.sharding import PartitionSpec as P

RATIO = 8
ACOUSTIC = 2
HALO = 8
SPLIT = 2

acoustic_substep = 0.2
drift_step = 0.4

MESH = pl.DeviceIdType.MESH


def kernel(
    sizes,
    height,
    wind,
    moisture,
    coeffs_hbm,
    damping_hbm,
    vmix_hbm,
    basis_hbm,
    edge_source_hbm,
    row_cell_hbm,
    col_cell_hbm,
    cond_rate_hbm,
    saturation_hbm,
    ancestry_hbm,
    height_out,
    wind_out,
    moisture_out,
    rain_out,
    coarse_out,
    coeffs_out,
    coeffs,
    damping,
    vmix,
    basis,
    edge_source,
    row_cell,
    col_cell,
    cond_rate,
    saturation,
    ancestry,
    st,
    cf,
    st_sel,
    cf_sel,
    st_relay,
    cur,
    rows_out,
    rows_in,
    packed,
    packed_in,
    diag_in,
    rim_part,
    rim_in,
    rim_z,
    rim_full,
    table,
    sides,
    sides_t,
    coarse_rows_buf,
    coarse_part,
    coarse_in,
    halo_recv,
    batch,
    mem_send,
    mem_recv,
    local,
    rounds,
):
    members, count_x, count_y = sizes
    plane = count_x * count_y
    levels = cur.shape[0]
    size_x = st.shape[2]
    size_y = st.shape[3]
    full_x = row_cell.shape[1]
    full_y = col_cell.shape[1]
    rim_points = basis.shape[1]
    coarse_x = coarse_out.shape[2]
    coarse_y = coarse_out.shape[3]
    share = rim_part.shape[1]
    f32 = jnp.float32

    z = lax.axis_index("mem")
    ix = lax.axis_index("gx")
    iy = lax.axis_index("gy")
    here = ix * count_y + iy
    low_side = z < 2
    inner = jnp.logical_and(z > 0, z < members - 1)
    outer = jnp.logical_not(inner)
    near = jnp.where(low_side, 1 - z, 5 - z)
    cross_inner = jnp.where(low_side, 2, 1)
    cross_outer = jnp.where(low_side, 3, 0)

    def plane_peer(step):
        other = lax.rem(here + step, plane)
        return other, other // count_y, lax.rem(other, count_y)

    own_slots = pl.ds(z * levels, levels)
    loads = [
        (height.at[0], st.at[own_slots, 0]),
        (wind.at[0, 0], st.at[own_slots, 1]),
        (wind.at[0, 1], st.at[own_slots, 2]),
        (moisture.at[0], st.at[own_slots, 3]),
        (coeffs_hbm, coeffs),
        (damping_hbm, damping),
        (vmix_hbm, vmix),
        (basis_hbm, basis),
        (edge_source_hbm, edge_source),
        (row_cell_hbm, row_cell),
        (col_cell_hbm, col_cell),
        (cond_rate_hbm, cond_rate),
        (saturation_hbm, saturation),
        (ancestry_hbm, ancestry),
    ]
    copies = [pltpu.make_async_copy(a, b, local.at[n]) for n, (a, b) in enumerate(loads)]
    for copy in copies:
        copy.start()

    def ready(*which):
        for n in which:
            copies[n].wait()

    if plane & (plane - 1):
        steps = [lax.rem(here + step, plane) for step in range(1, plane)]
        n_rounds = 2
    else:
        n_dims = plane.bit_length() - 1
        n_rounds = max(n_dims - 1, 2)
        steps = []
        for k in range(n_dims):
            bit = lax.rem(here // 2**k, 2)
            steps.append(here + 2**k * (1 - 2 * bit))

    def greet(sem, n):
        for other in steps:
            pl.semaphore_signal(
                sem,
                inc=1,
                device_id=(z, other // count_y, lax.rem(other, count_y)),
                device_id_type=MESH,
            )
        pl.semaphore_signal(sem, inc=1, device_id=(near, ix, iy), device_id_type=MESH)

        @pl.when(inner)
        def _():
            for other in (cross_inner, cross_outer)[:n]:
                pl.semaphore_signal(
                    sem, inc=1, device_id=(other, ix, iy), device_id_type=MESH
                )

    barrier = pltpu.get_barrier_semaphore()
    greet(barrier, 2)

    ready(0, 1, 2, 3)

    pl.semaphore_wait(barrier, len(steps) + 2)
    greet(rounds.at[0], 1)

    pieces = [(0, pl.ds(0, 4)), (1, pl.ds(0, 2)), (1, pl.ds(2, 2))]
    pieces += [(l, pl.ds(0, 4)) for l in range(2, levels)]
    n_pieces = len(pieces)

    def chunk(c, slot):
        if c >= n_pieces:
            return cf.at[slot * 2 + c - n_pieces]
        return st.at[slot * levels + pieces[c][0], pieces[c][1]]

    def chosen(c, way):
        if c >= n_pieces:
            return cf_sel.at[way, c - n_pieces]
        return st_sel.at[way, pieces[c][0], pieces[c][1]]

    def z_copy(c, kind, src, slot, target):
        return pltpu.make_async_remote_copy(
            src_ref=src,
            dst_ref=chunk(c, slot),
            send_sem=mem_send.at[0 if c < n_pieces else 1],
            recv_sem=mem_recv.at[kind if c == 0 else 1 + 2 * c + kind],
            device_id=(target, ix, iy),
            device_id_type=MESH,
        )

    def own_near(c):
        return z_copy(c, 0, chunk(c, z), z, near)

    def own_cross(c):
        return z_copy(c, jnp.where(outer, 2, 1), chunk(c, z), z, cross_inner)

    def sel_inner(c):
        return z_copy(c, 1, chosen(c, 0), z, cross_inner)

    def sel_outer(c):
        return z_copy(c, 1, chosen(c, 1), z, cross_outer)

    def relay_near(c):
        return z_copy(c, 0, st_relay, z, near)

    def arrived(c, kind, slot):
        z_copy(c, kind, chunk(c, slot), slot, near).wait_recv()

    first, rest = 0, list(range(1, n_pieces))
    specs = [n_pieces, n_pieces + 1]
    lead, later = rest[:2], rest[2:]

    @pl.when(inner)
    def _():
        own_cross(first).start()
        for c in rest:
            own_near(c).start()

    @pl.when(outer)
    def _():
        for c in lead:
            own_near(c).start()
        own_cross(first).start()
        for c in later:
            own_near(c).start()

    ready(4, 5, 6)
    new_fields = []
    for f in range(4):
        c = coeffs[0, f]
        acc = vmix[:, 0:1] * c[0:1]
        for j in range(1, levels):
            acc = acc + vmix[:, j : j + 1] * c[j : j + 1]
        new_fields.append(acc * damping[...])
    for f in range(4):
        cf[2 * z + f // 2, f % 2] = new_fields[f]
    pl.semaphore_wait(rounds.at[0], len(steps) + jnp.where(inner, 2, 1))
    for k in range(1, n_rounds):
        greet(rounds.at[k], 0)
        if k < n_rounds - 1:
            pl.semaphore_wait(rounds.at[k], len(steps) + 1)
    low = jnp.concatenate(new_fields, axis=0).astype(jnp.bfloat16)
    ready(7)
    part = jnp.dot(low, basis[...], preferred_element_type=f32)
    for g in range(count_x):
        rim_part[g] = part[g * share : (g + 1) * share]

    def rim_copy(step):
        _, px, py = plane_peer(step)
        return pltpu.make_async_remote_copy(
            src_ref=rim_part.at[px],
            dst_ref=rim_in.at[here],
            send_sem=batch.at[0],
            recv_sem=batch.at[1],
            device_id=(z, px, py),
            device_id_type=MESH,
        )

    pl.semaphore_wait(rounds.at[n_rounds - 1], len(steps) + 1)
    for step in range(1, plane):
        rim_copy(step).start()

    ready(8, 9, 10, 11, 12, 13)
    mine = ancestry[z]

    def select_near(c):
        arrived(c, 0, near)
        for way, target in ((0, cross_inner), (1, cross_outer)):
            take_own = ancestry[target] != near
            chosen(c, way)[...] = jnp.where(take_own, chunk(c, z)[...], chunk(c, near)[...])

    n_edge = edge_source.shape[0]
    table[...] = (
        (lax.broadcasted_iota(jnp.int32, (rim_points, n_edge), 0)
         == edge_source[...].reshape(1, n_edge))
        .astype(f32)
        .astype(jnp.bfloat16)
    )
    row_table = (
        lax.broadcasted_iota(jnp.int32, (coarse_x, full_x), 0) == row_cell[...]
    ).astype(f32)
    row_count = jnp.sum(row_table, axis=1, keepdims=True)
    wide = lax.rem(
        lax.broadcasted_iota(jnp.int32, (levels * coarse_y, full_y), 0), coarse_y
    )
    col_table = (wide == col_cell[...]).astype(f32)
    col_count = lax.dot_general(
        jnp.ones((8, full_y), f32),
        col_table,
        (((1,), (1,)), ((), ())),
        preferred_element_type=f32,
    )[0:1]
    col_off = pl.multiple_of(iy * size_y, 128)
    row_off = pl.multiple_of(ix * size_x, 8)
    cells_here = col_cell[:, pl.ds(col_off, size_y)]
    wide_here = lax.broadcasted_iota(jnp.int32, (levels * coarse_y, size_y), 0)
    coarse_rows_buf[...] = jnp.zeros_like(coarse_rows_buf)

    @pl.when(inner)
    def _():
        for c in lead:
            select_near(c)
            sel_outer(c).start()
            sel_inner(c).start()

    def batch_of(n, ref, count):
        many = ref.at[pl.ds(0, count)]
        return pltpu.make_async_remote_copy(
            src_ref=many,
            dst_ref=many,
            send_sem=batch.at[n],
            recv_sem=batch.at[n + 1],
            device_id=(near, ix, iy),
            device_id_type=MESH,
        )

    batch_of(0, rim_in, plane - 1).wait_recv()
    total = rim_part[ix]
    for step in range(1, plane):
        other, _, _ = plane_peer(step)
        total = total + rim_in[other]
    rim_z[z] = total

    def rimz_copy(step, source):
        return pltpu.make_async_remote_copy(
            src_ref=rim_z.at[source],
            dst_ref=rim_z.at[source],
            send_sem=batch.at[2],
            recv_sem=batch.at[3],
            device_id=(lax.rem(z + step, members), ix, iy),
            device_id_type=MESH,
        )

    for step in range(1, members):
        rimz_copy(step, z).start()

    @pl.when(outer)
    def _():
        for c in [first] + specs:
            own_near(c).start()

    @pl.when(inner)
    def _():
        arrived(first, 1, cross_inner)
        arrived(first, 2, cross_outer)
        want = ancestry[near]
        a = chunk(first, z)[...]
        a = jnp.where(want == cross_inner, chunk(first, cross_inner)[...], a)
        st_relay[...] = jnp.where(want == cross_outer, chunk(first, cross_outer)[...], a)
        relay_near(first).start()
        for c in later:
            select_near(c)
            sel_outer(c).start()
        for c in later:
            sel_inner(c).start()

    batch_of(2, rim_z, members - 1).wait_recv()
    share_sel = rim_z[z]
    for step in range(1, members):
        source = lax.rem(z + step, members)
        share_sel = jnp.where(mine == source, rim_z[source], share_sel)
    rim_full[ix] = share_sel

    def rimg_copy(step, source):
        return pltpu.make_async_remote_copy(
            src_ref=rim_full.at[source],
            dst_ref=rim_full.at[source],
            send_sem=batch.at[4],
            recv_sem=batch.at[5],
            device_id=(z, lax.rem(ix + step, count_x), iy),
            device_id_type=MESH,
        )

    for step in range(1, count_x):
        rimg_copy(step, ix).start()

    @pl.when(inner)
    def _():
        arrived(first, 0, near)
        for c in specs:
            own_near(c).start()

    lane = lax.broadcasted_iota(jnp.int32, (size_x, size_y), 1)
    width = size_y // (4 * levels)
    half = width // 2

    def settle(c, ref):
        arrived(c, 1, cross_inner)

        @pl.when(outer)
        def _():
            arrived(c, 0, near)

        a = jnp.where(mine == z, chunk(c, z)[...], chunk(c, cross_inner)[...])
        ref[...] = jnp.where(mine == near, chunk(c, near)[...], a)

    order = list(range(1, levels - 1)) + [first, levels - 1]
    groups = [order[:SPLIT], order[SPLIT:]]

    def halo_jobs(g, mode):
        lev = pl.ds(SPLIT * g, len(groups[g]))
        for dx in (-1, 0, 1):
            for dy in (-1, 0, 1):
                if dx == 0 and dy == 0:
                    continue
                flip = -1 if mode == "recv" else 1
                ok = jnp.bool_(True)
                if dx * flip == -1:
                    ok = jnp.logical_and(ok, ix > 0)
                if dx * flip == 1:
                    ok = jnp.logical_and(ok, ix < count_x - 1)
                if dy * flip == -1:
                    ok = jnp.logical_and(ok, iy > 0)
                if dy * flip == 1:
                    ok = jnp.logical_and(ok, iy < count_y - 1)
                sx = 0 if dx == -1 else 1
                sy = 0 if dy == -1 else 1
                rows = pl.ds(0, HALO) if dx == -1 else pl.ds(size_x - HALO, HALO)
                if dy == 0:
                    src, dst, base = rows_out.at[sx, lev], rows_in.at[sx, lev], sx
                elif dx == 0:
                    src, dst, base = packed.at[g], packed_in.at[g, sy], 2 + sy
                else:
                    src, dst = packed.at[g, rows, :], diag_in.at[g, sx, sy]
                    base = 4 + 2 * sx + sy

                def go(src=src, dst=dst, base=base, target=(z, ix + dx, iy + dy)):
                    copy = pltpu.make_async_remote_copy(
                        src_ref=src,
                        dst_ref=dst,
                        send_sem=local.at[8 * g + base],
                        recv_sem=halo_recv.at[8 * g + base],
                        device_id=target,
                        device_id_type=MESH,
                    )
                    if mode == "start":
                        copy.start()
                    elif mode == "send":
                        copy.wait_send()
                    else:
                        copy.wait_recv()

                pl.when(ok)(go)

    def halo_out(g):
        pack = jnp.zeros((size_x, size_y), f32)
        for l in groups[g]:
            if l != first:
                for c in range(n_pieces):
                    if pieces[c][0] == l:
                        settle(c, cur.at[l, pieces[c][1]])
            for f in range(4):
                rows_out[0, order.index(l), f] = cur[l, f, 0:HALO]
                rows_out[1, order.index(l), f] = cur[l, f, size_x - HALO :]
                k = f * levels + l
                moved = pltpu.roll(cur[l, f], (width * k + half) % size_y, 1)
                pack = jnp.where(lane // width == k, moved, pack)
        packed[g] = pack
        halo_jobs(g, "start")

    halo_out(0)

    @pl.when(inner)
    def _():
        for c in specs:
            select_near(c)
            sel_outer(c).start()
        for c in specs:
            sel_inner(c).start()

    @pl.when(outer)
    def _():
        arrived(first, 0, near)
        cur[first] = jnp.where(mine == z, chunk(first, z)[...], chunk(first, near)[...])

    @pl.when(inner)
    def _():
        a = chunk(first, cross_outer)[...]
        a = jnp.where(mine == cross_inner, chunk(first, cross_inner)[...], a)
        a = jnp.where(mine == near, chunk(first, near)[...], a)
        cur[first] = jnp.where(mine == z, chunk(first, z)[...], a)

    halo_out(1)

    ext_x = size_x + 2 * HALO
    ext_y = 2 * size_y
    rpos = lax.broadcasted_iota(jnp.int32, (ext_x, ext_y), 0)
    cpos = lax.broadcasted_iota(jnp.int32, (ext_x, ext_y), 1)
    gx_pos = ix * size_x + jnp.where(rpos < size_x + HALO, rpos, rpos - ext_x)
    gy_pos = iy * size_y + jnp.where(cpos < size_y + size_y // 2, cpos, cpos - ext_y)
    inside = (gx_pos >= 0) & (gx_pos < full_x) & (gy_pos >= 0) & (gy_pos < full_y)
    at_west = gx_pos == -1
    at_east = gx_pos == full_x
    at_south = gy_pos == -1

    batch_of(4, rim_full, count_x - 1).wait_recv()
    rim = jnp.concatenate([rim_full[g] for g in range(count_x)], axis=0)
    rim_hi = rim.astype(jnp.bfloat16)
    rim_lo = (rim - rim_hi.astype(f32)).astype(jnp.bfloat16)
    both = jnp.dot(
        jnp.concatenate([rim_hi, rim_lo], axis=0), table[...], preferred_element_type=f32
    )
    n_rows = 4 * levels
    edge = both[0:n_rows] + both[n_rows:]
    sides[...] = edge
    for s in range(2):
        begin = 2 * full_y + s * full_x
        sides_t[s, HALO : HALO + full_x, :] = edge[:, begin : begin + full_x].T
        sides_t[s, 0:HALO, :] = jnp.zeros((HALO, n_rows), f32)
        sides_t[s, HALO + full_x :, :] = jnp.zeros((HALO, n_rows), f32)
    lane1 = lax.broadcasted_iota(jnp.int32, (n_rows, size_y), 1)

    def x_side(begin):
        own = sides[:, pl.ds(pl.multiple_of(begin + col_off, 128), size_y)]
        after = lax.rem(iy + 1, count_y) * size_y
        before = lax.rem(iy + count_y - 1, count_y) * size_y
        nxt_b = sides[:, pl.ds(pl.multiple_of(begin + after, 128), size_y)]
        prv_b = sides[:, pl.ds(pl.multiple_of(begin + before, 128), size_y)]
        return jnp.concatenate([own, jnp.where(lane1 < size_y // 2, nxt_b, prv_b)], axis=1)

    def y_side(s):
        body_rows = sides_t[s, pl.ds(pl.multiple_of(row_off + HALO, 8), size_x), :]
        above = sides_t[s, pl.ds(pl.multiple_of(row_off + HALO + size_x, 8), HALO), :]
        below = sides_t[s, pl.ds(row_off, HALO), :]
        return jnp.concatenate([body_rows, above, below], axis=0)

    west, east = x_side(0), x_side(full_y)
    south, north = y_side(0), y_side(1)

    lane2 = lax.broadcasted_iota(jnp.int32, (size_x + 2 * HALO, size_y), 1)
    take_next = lax.rem(lane2, width) >= half
    rains = {}
    for l in order:
        at = order.index(l)
        g = at // SPLIT
        if l == groups[g][0]:
            halo_jobs(g, "recv")
            nxt = jnp.concatenate([packed_in[g, 0], diag_in[g, 0, 0], diag_in[g, 1, 0]], axis=0)
            prv = jnp.concatenate([packed_in[g, 1], diag_in[g, 0, 1], diag_in[g, 1, 1]], axis=0)
            mixed = jnp.where(take_next, nxt, prv)

        def extended(f):
            k = f * levels + l
            left = jnp.concatenate([cur[l, f], rows_in[0, at, f], rows_in[1, at, f]], axis=0)
            right = pltpu.roll(mixed, (size_y - (width * k + half)) % size_y, 1)
            return jnp.concatenate([left, right], axis=1)

        def outside(f):
            k = f * levels + l
            value = jnp.where(at_south, south[:, k : k + 1], north[:, k : k + 1])
            value = jnp.where(at_east, east[k : k + 1], value)
            return jnp.where(at_west, west[k : k + 1], value)

        def up(a):
            return pltpu.roll(a, ext_x - 1, 0)

        def down(a):
            return pltpu.roll(a, 1, 0)

        def right_of(a):
            return pltpu.roll(a, ext_y - 1, 1)

        def left_of(a):
            return pltpu.roll(a, 1, 1)

        bh, bu, bv, bq = outside(0), outside(1), outside(2), outside(3)
        h, u, v, q = extended(0), extended(1), extended(2), extended(3)
        h = jnp.where(inside, h, bh)
        q = jnp.where(inside, q, bq)
        for substep in range(ACOUSTIC):
            u = u - acoustic_substep * (up(h) - down(h))
            v = v - acoustic_substep * (right_of(h) - left_of(h))
            u = jnp.where(inside, u, bu)
            v = jnp.where(inside, v, bv)
            h = h - acoustic_substep * ((up(u) - down(u)) + (right_of(v) - left_of(v)))
            h = jnp.where(inside, h, bh)
        flux = (
            jnp.maximum(u, 0.0) * (q - down(q)) + jnp.minimum(u, 0.0) * (up(q) - q)
        ) + (
            jnp.maximum(v, 0.0) * (q - left_of(q)) + jnp.minimum(v, 0.0) * (right_of(q) - q)
        )
        q = (q - drift_step * flux)[0:size_x, 0:size_y]
        fallen = cond_rate[l] * jnp.maximum(q - saturation[l], 0.0)
        q_new = q - fallen
        height_out[0, l] = h[0:size_x, 0:size_y]
        wind_out[0, 0, l] = u[0:size_x, 0:size_y]
        wind_out[0, 1, l] = v[0:size_x, 0:size_y]
        moisture_out[0, l] = q_new
        rains[l] = fallen
        spread = ((wide_here - l * coarse_y) == cells_here).astype(f32)
        summed = lax.dot_general(
            q_new,
            spread,
            (((1,), (1,)), ((), ())),
            precision=lax.Precision.HIGHEST,
            preferred_element_type=f32,
        )
        rows_here = pl.ds(row_off, size_x)
        coarse_rows_buf[rows_here, :] = coarse_rows_buf[rows_here, :] + summed

    coarse_part[...] = jnp.dot(
        row_table,
        coarse_rows_buf[...],
        precision=lax.Precision.HIGHEST,
        preferred_element_type=f32,
    )

    def crs_copy(step, source):
        _, px, py = plane_peer(step)
        return pltpu.make_async_remote_copy(
            src_ref=coarse_part,
            dst_ref=coarse_in.at[source],
            send_sem=batch.at[6],
            recv_sem=batch.at[7],
            device_id=(z, px, py),
            device_id_type=MESH,
        )

    for step in range(1, plane):
        crs_copy(step, here).start()
    rain = rains[0]
    for l in range(1, levels):
        rain = rain + rains[l]
    rain_out[0] = rain

    for half_at, c in enumerate(specs):
        settle(c, coeffs_out.at[0, pl.ds(2 * half_at, 2)])

    batch_of(6, coarse_in, plane - 1).wait_recv()
    total = coarse_part[...]
    for step in range(1, plane):
        other, _, _ = plane_peer(step)
        total = total + coarse_in[other]
    total = total / (row_count * col_count)
    for l in range(levels):
        coarse_out[0, l] = total[:, l * coarse_y : (l + 1) * coarse_y]

    for g in range(2):
        halo_jobs(g, "send")
    batch_of(0, rim_in, plane - 1).wait_send()
    batch_of(2, rim_z, members - 1).wait_send()
    batch_of(4, rim_full, count_x - 1).wait_send()
    batch_of(6, coarse_in, plane - 1).wait_send()

    def sent(n, ref, count):
        many = ref.at[pl.ds(0, count)]
        pltpu.make_async_remote_copy(
            src_ref=many,
            dst_ref=many,
            send_sem=mem_send.at[n],
            recv_sem=mem_recv.at[0],
            device_id=(near, ix, iy),
            device_id_type=MESH,
        ).wait_send()

    @pl.when(outer)
    def _():
        sent(0, st, levels + 1)
        sent(1, cf, 2)

    @pl.when(inner)
    def _():
        sent(0, st, 3 * levels - 1)
        sent(1, cf, 6)


def write_out(*refs):
    sems = refs[12]
    copies = [pltpu.make_async_copy(refs[n], refs[6 + n], sems.at[n]) for n in range(6)]
    for copy in copies:
        copy.start()
    for copy in copies:
        copy.wait()


def body(
    sizes,
    height,
    wind,
    moisture,
    coeffs,
    damping,
    vmix,
    basis,
    edge_source,
    row_cell,
    col_cell,
    cond_rate,
    saturation,
    ancestry,
):
    members, count_x, count_y = sizes
    plane = count_x * count_y
    _, levels, size_x, size_y = height.shape
    local_k = coeffs.shape[3]
    rim_points = basis.shape[1]
    full_x = row_cell.shape[0]
    full_y = col_cell.shape[0]
    n_edge = edge_source.shape[0]
    coarse_x, coarse_y = full_x // RATIO, full_y // RATIO
    share = 4 * levels // count_x
    rows = 4 * levels
    f32 = jnp.float32
    vmem = pl.BlockSpec(memory_space=pltpu.VMEM)
    dma = pltpu.SemaphoreType.DMA
    coarse_chunk = (coarse_x, levels * coarse_y)
    operands = (
        height,
        wind,
        moisture,
        coeffs,
        damping.reshape(1, -1),
        vmix,
        basis,
        edge_source,
        row_cell.reshape(1, -1),
        col_cell.reshape(1, -1),
        cond_rate,
        saturation,
        ancestry,
    )
    chunks = levels + 3
    scratch = [
        *[pltpu.VMEM(a.shape, a.dtype) for a in operands[3:10]],
        *[pltpu.SMEM(a.shape, a.dtype) for a in operands[10:]],
        pltpu.VMEM((members * levels, 4, size_x, size_y), f32),
        pltpu.VMEM((members * 2, 2, levels, local_k), f32),
        pltpu.VMEM((2, levels, 4, size_x, size_y), f32),
        pltpu.VMEM((2, 2, 2, levels, local_k), f32),
        pltpu.VMEM((4, size_x, size_y), f32),
        pltpu.VMEM((levels, 4, size_x, size_y), f32),
        pltpu.VMEM((2, levels, 4, HALO, size_y), f32),
        pltpu.VMEM((2, levels, 4, HALO, size_y), f32),
        pltpu.VMEM((2, size_x, size_y), f32),
        pltpu.VMEM((2, 2, size_x, size_y), f32),
        pltpu.VMEM((2, 2, 2, HALO, size_y), f32),
        pltpu.VMEM((count_x, share, rim_points), f32),
        pltpu.VMEM((plane, share, rim_points), f32),
        pltpu.VMEM((members, share, rim_points), f32),
        pltpu.VMEM((count_x, share, rim_points), f32),
        pltpu.VMEM((rim_points, n_edge), jnp.bfloat16),
        pltpu.VMEM((rows, n_edge), f32),
        pltpu.VMEM((2, full_x + 2 * HALO, rows), f32),
        pltpu.VMEM((full_x, levels * coarse_y), f32),
        pltpu.VMEM(coarse_chunk, f32),
        pltpu.VMEM((plane, *coarse_chunk), f32),
        dma((16,)),
        dma((8,)),
        dma((2,)),
        dma((1 + 2 * chunks,)),
        dma((16,)),
        pltpu.SemaphoreType.REGULAR((max(plane.bit_length() - 2, 2),)),
    ]
    outs = (
        pltpu.VMEM(height.shape, f32),
        pltpu.VMEM(wind.shape, f32),
        pltpu.VMEM(moisture.shape, f32),
        pltpu.VMEM((1, size_x, size_y), f32),
        pltpu.VMEM((1, levels, coarse_x, coarse_y), f32),
        pltpu.VMEM(coeffs.shape, f32),
    )
    results = pl.pallas_call(
        functools.partial(kernel, sizes),
        out_shape=outs,
        in_specs=[pl.BlockSpec(memory_space=pltpu.HBM)] * 13,
        out_specs=(vmem,) * 6,
        scratch_shapes=scratch,
        compiler_params=pltpu.CompilerParams(
            collective_id=0, has_side_effects=True, vmem_limit_bytes=36 * 1024 * 1024
        ),
    )(*[pltpu.with_memory_space_constraint(a, pltpu.HBM) for a in operands])
    return pl.pallas_call(
        write_out,
        out_shape=tuple(jax.ShapeDtypeStruct(r.shape, f32) for r in results),
        in_specs=[vmem] * 6,
        out_specs=(pl.BlockSpec(memory_space=pl.ANY),) * 6,
        scratch_shapes=[dma((6,))],
        compiler_params=pltpu.CompilerParams(vmem_limit_bytes=8 * 1024 * 1024),
    )(*results)


def solution(mesh):
    sizes = (mesh.shape["mem"], mesh.shape["gx"], mesh.shape["gy"])
    in_specs = (
        P("mem", None, "gx", "gy"),
        P("mem", None, None, "gx", "gy"),
        P("mem", None, "gx", "gy"),
        P("mem", None, None, ("gx", "gy")),
        P(("gx", "gy")),
        P(),
        P(("gx", "gy"), None),
        P(),
        P(),
        P(),
        P(),
        P(),
        P(),
    )
    out_specs = (
        P("mem", None, "gx", "gy"),
        P("mem", None, None, "gx", "gy"),
        P("mem", None, "gx", "gy"),
        P("mem", "gx", "gy"),
        P("mem", None, None, None),
        P("mem", None, None, ("gx", "gy")),
    )
    return jax.shard_map(
        functools.partial(body, sizes),
        mesh=mesh,
        in_specs=in_specs,
        out_specs=out_specs,
        check_vma=False,
    )
```

```python
import functools

import jax
import jax.numpy as jnp
from jax import lax
from jax.experimental import pallas as pl
from jax.experimental.pallas import tpu as pltpu
from jax.sharding import PartitionSpec as P

RATIO = 8
ACOUSTIC = 2
HALO = 8
SPLIT = 2

acoustic_substep = 0.2
drift_step = 0.4

MESH = pl.DeviceIdType.MESH


def kernel(
    sizes,
    height,
    wind,
    moisture,
    coeffs_hbm,
    damping_hbm,
    vmix_hbm,
    basis_hbm,
    edge_source_hbm,
    row_cell_hbm,
    col_cell_hbm,
    cond_rate_hbm,
    saturation_hbm,
    ancestry_hbm,
    height_out,
    wind_out,
    moisture_out,
    rain_out,
    coarse_out,
    coeffs_out,
    coeffs,
    damping,
    vmix,
    basis,
    edge_source,
    row_cell,
    col_cell,
    cond_rate,
    saturation,
    ancestry,
    st,
    cf,
    st_sel,
    cf_sel,
    st_relay,
    cur,
    rows_out,
    rows_in,
    packed,
    packed_in,
    diag_in,
    rim_part,
    rim_in,
    rim_z,
    rim_full,
    table,
    sides,
    sides_t,
    spread,
    row_table3,
    coarse_rows_buf,
    coarse_part,
    coarse_in,
    halo_recv,
    batch,
    mem_send,
    mem_recv,
    local,
    rounds,
):
    members, count_x, count_y = sizes
    plane = count_x * count_y
    levels = cur.shape[0]
    size_x = st.shape[2]
    size_y = st.shape[3]
    full_x = row_cell.shape[1]
    full_y = col_cell.shape[1]
    rim_points = basis.shape[1]
    coarse_x = coarse_out.shape[2]
    coarse_y = coarse_out.shape[3]
    share = rim_part.shape[1]
    f32 = jnp.float32

    z = lax.axis_index("mem")
    ix = lax.axis_index("gx")
    iy = lax.axis_index("gy")
    here = ix * count_y + iy
    low_side = z < 2
    inner = jnp.logical_and(z > 0, z < members - 1)
    outer = jnp.logical_not(inner)
    near = jnp.where(low_side, 1 - z, 5 - z)
    cross_inner = jnp.where(low_side, 2, 1)
    cross_outer = jnp.where(low_side, 3, 0)

    def plane_peer(step):
        other = lax.rem(here + step, plane)
        return other, other // count_y, lax.rem(other, count_y)

    own_slots = pl.ds(z * levels, levels)
    loads = [
        (height.at[0], st.at[own_slots, 0]),
        (wind.at[0, 0], st.at[own_slots, 1]),
        (wind.at[0, 1], st.at[own_slots, 2]),
        (moisture.at[0], st.at[own_slots, 3]),
        (coeffs_hbm, coeffs),
        (damping_hbm, damping),
        (vmix_hbm, vmix),
        (basis_hbm, basis),
        (edge_source_hbm, edge_source),
        (row_cell_hbm, row_cell),
        (col_cell_hbm, col_cell),
        (cond_rate_hbm, cond_rate),
        (saturation_hbm, saturation),
        (ancestry_hbm, ancestry),
    ]
    copies = [pltpu.make_async_copy(a, b, local.at[n]) for n, (a, b) in enumerate(loads)]
    for copy in copies:
        copy.start()

    def ready(*which):
        for n in which:
            copies[n].wait()

    if plane & (plane - 1):
        steps = [lax.rem(here + step, plane) for step in range(1, plane)]
        n_rounds = 2
    else:
        n_dims = plane.bit_length() - 1
        n_rounds = max(n_dims - 1, 2)
        steps = []
        for k in range(n_dims):
            bit = lax.rem(here // 2**k, 2)
            steps.append(here + 2**k * (1 - 2 * bit))

    def greet(sem, n):
        for other in steps:
            pl.semaphore_signal(
                sem,
                inc=1,
                device_id=(z, other // count_y, lax.rem(other, count_y)),
                device_id_type=MESH,
            )
        pl.semaphore_signal(sem, inc=1, device_id=(near, ix, iy), device_id_type=MESH)

        @pl.when(inner)
        def _():
            for other in (cross_inner, cross_outer)[:n]:
                pl.semaphore_signal(
                    sem, inc=1, device_id=(other, ix, iy), device_id_type=MESH
                )

    barrier = pltpu.get_barrier_semaphore()
    greet(barrier, 2)

    ready(0, 1, 2, 3)

    pl.semaphore_wait(barrier, len(steps) + 2)
    greet(rounds.at[0], 1)

    pieces = [(0, pl.ds(0, 4)), (1, pl.ds(0, 2)), (1, pl.ds(2, 2))]
    pieces += [(l, pl.ds(0, 4)) for l in range(2, levels)]
    n_pieces = len(pieces)

    def chunk(c, slot):
        if c >= n_pieces:
            return cf.at[slot * 2 + c - n_pieces]
        return st.at[slot * levels + pieces[c][0], pieces[c][1]]

    def chosen(c, way):
        if c >= n_pieces:
            return cf_sel.at[way, c - n_pieces]
        return st_sel.at[way, pieces[c][0], pieces[c][1]]

    def z_copy(c, kind, src, slot, target):
        return pltpu.make_async_remote_copy(
            src_ref=src,
            dst_ref=chunk(c, slot),
            send_sem=mem_send.at[0 if c < n_pieces else 1],
            recv_sem=mem_recv.at[kind if c == 0 else 1 + 2 * c + kind],
            device_id=(target, ix, iy),
            device_id_type=MESH,
        )

    def own_near(c):
        return z_copy(c, 0, chunk(c, z), z, near)

    def own_cross(c):
        return z_copy(c, jnp.where(outer, 2, 1), chunk(c, z), z, cross_inner)

    def sel_inner(c):
        return z_copy(c, 1, chosen(c, 0), z, cross_inner)

    def sel_outer(c):
        return z_copy(c, 1, chosen(c, 1), z, cross_outer)

    def relay_near(c):
        return z_copy(c, 0, st_relay, z, near)

    def arrived(c, kind, slot):
        z_copy(c, kind, chunk(c, slot), slot, near).wait_recv()

    first, rest = 0, list(range(1, n_pieces))
    specs = [n_pieces, n_pieces + 1]
    lead, later = rest[:2], rest[2:]

    @pl.when(inner)
    def _():
        own_cross(first).start()
        for c in rest:
            own_near(c).start()

    @pl.when(outer)
    def _():
        for c in lead:
            own_near(c).start()
        own_cross(first).start()
        for c in later:
            own_near(c).start()

    ready(4, 5, 6)
    new_fields = []
    for f in range(4):
        c = coeffs[0, f]
        acc = vmix[:, 0:1] * c[0:1]
        for j in range(1, levels):
            acc = acc + vmix[:, j : j + 1] * c[j : j + 1]
        new_fields.append(acc * damping[...])
    for f in range(4):
        cf[2 * z + f // 2, f % 2] = new_fields[f]
    pl.semaphore_wait(rounds.at[0], len(steps) + jnp.where(inner, 2, 1))
    for k in range(1, n_rounds):
        greet(rounds.at[k], 0)
        if k < n_rounds - 1:
            pl.semaphore_wait(rounds.at[k], len(steps) + 1)
    low = jnp.concatenate(new_fields, axis=0).astype(jnp.bfloat16)
    ready(7)
    part = jnp.dot(low, basis[...], preferred_element_type=f32)
    for g in range(count_x):
        rim_part[g] = part[g * share : (g + 1) * share]

    def rim_copy(step):
        _, px, py = plane_peer(step)
        return pltpu.make_async_remote_copy(
            src_ref=rim_part.at[px],
            dst_ref=rim_in.at[here],
            send_sem=batch.at[0],
            recv_sem=batch.at[1],
            device_id=(z, px, py),
            device_id_type=MESH,
        )

    pl.semaphore_wait(rounds.at[n_rounds - 1], len(steps) + 1)
    for step in range(1, plane):
        rim_copy(step).start()

    ready(8, 9, 10, 11, 12, 13)
    mine = ancestry[z]

    def select_near(c):
        arrived(c, 0, near)
        for way, target in ((0, cross_inner), (1, cross_outer)):
            take_own = ancestry[target] != near
            chosen(c, way)[...] = jnp.where(take_own, chunk(c, z)[...], chunk(c, near)[...])

    n_edge = edge_source.shape[0]
    table[...] = (
        (lax.broadcasted_iota(jnp.int32, (rim_points, n_edge), 0)
         == edge_source[...].reshape(1, n_edge))
        .astype(f32)
        .astype(jnp.bfloat16)
    )
    row_table = (
        lax.broadcasted_iota(jnp.int32, (coarse_x, full_x), 0) == row_cell[...]
    ).astype(f32)
    row_count = jnp.sum(row_table, axis=1, keepdims=True)
    wide = lax.rem(
        lax.broadcasted_iota(jnp.int32, (levels * coarse_y, full_y), 0), coarse_y
    )
    col_table = (wide == col_cell[...]).astype(f32)
    col_count = lax.dot_general(
        jnp.ones((8, full_y), f32),
        col_table,
        (((1,), (1,)), ((), ())),
        preferred_element_type=f32,
    )[0:1]
    col_off = pl.multiple_of(iy * size_y, 128)
    row_off = pl.multiple_of(ix * size_x, 8)
    cells_here = col_cell[:, pl.ds(col_off, size_y)]
    wide_here = lax.broadcasted_iota(jnp.int32, (levels * coarse_y, size_y), 0)
    coarse_rows_buf[...] = jnp.zeros_like(coarse_rows_buf)
    for m in range(3):
        row_table3[:, m * full_x : (m + 1) * full_x] = row_table.astype(jnp.bfloat16)

    @pl.when(inner)
    def _():
        for c in lead:
            select_near(c)
            sel_outer(c).start()
            sel_inner(c).start()

    def batch_of(n, ref, count):
        many = ref.at[pl.ds(0, count)]
        return pltpu.make_async_remote_copy(
            src_ref=many,
            dst_ref=many,
            send_sem=batch.at[n],
            recv_sem=batch.at[n + 1],
            device_id=(near, ix, iy),
            device_id_type=MESH,
        )

    batch_of(0, rim_in, plane - 1).wait_recv()
    total = rim_part[ix]
    for step in range(1, plane):
        other, _, _ = plane_peer(step)
        total = total + rim_in[other]
    rim_z[z] = total

    def rimz_copy(step, source):
        return pltpu.make_async_remote_copy(
            src_ref=rim_z.at[source],
            dst_ref=rim_z.at[source],
            send_sem=batch.at[2],
            recv_sem=batch.at[3],
            device_id=(lax.rem(z + step, members), ix, iy),
            device_id_type=MESH,
        )

    for step in range(1, members):
        rimz_copy(step, z).start()

    @pl.when(outer)
    def _():
        for c in [first] + specs:
            own_near(c).start()

    @pl.when(inner)
    def _():
        arrived(first, 1, cross_inner)
        arrived(first, 2, cross_outer)
        want = ancestry[near]
        a = chunk(first, z)[...]
        a = jnp.where(want == cross_inner, chunk(first, cross_inner)[...], a)
        st_relay[...] = jnp.where(want == cross_outer, chunk(first, cross_outer)[...], a)
        relay_near(first).start()
        for c in later:
            select_near(c)
            sel_outer(c).start()
        for c in later:
            sel_inner(c).start()

    batch_of(2, rim_z, members - 1).wait_recv()
    share_sel = rim_z[z]
    for step in range(1, members):
        source = lax.rem(z + step, members)
        share_sel = jnp.where(mine == source, rim_z[source], share_sel)
    rim_full[ix] = share_sel

    def rimg_copy(step, source):
        return pltpu.make_async_remote_copy(
            src_ref=rim_full.at[source],
            dst_ref=rim_full.at[source],
            send_sem=batch.at[4],
            recv_sem=batch.at[5],
            device_id=(z, lax.rem(ix + step, count_x), iy),
            device_id_type=MESH,
        )

    for step in range(1, count_x):
        rimg_copy(step, ix).start()

    @pl.when(inner)
    def _():
        arrived(first, 0, near)
        for c in specs:
            own_near(c).start()

    lane = lax.broadcasted_iota(jnp.int32, (size_x, size_y), 1)
    width = size_y // (4 * levels)
    half = width // 2

    def settle(c, ref):
        arrived(c, 1, cross_inner)

        @pl.when(outer)
        def _():
            arrived(c, 0, near)

        a = jnp.where(mine == z, chunk(c, z)[...], chunk(c, cross_inner)[...])
        ref[...] = jnp.where(mine == near, chunk(c, near)[...], a)

    order = list(range(1, levels - 1)) + [first, levels - 1]
    groups = [order[:SPLIT], order[SPLIT:]]
    for n, l in enumerate(order):
        hit = ((wide_here - l * coarse_y) == cells_here).astype(f32).astype(jnp.bfloat16)
        for m in range(3):
            spread[:, (3 * n + m) * size_y : (3 * n + m + 1) * size_y] = hit

    def halo_jobs(g, mode):
        lev = pl.ds(SPLIT * g, len(groups[g]))
        toward = [(-1, -1), (0, -1), (-1, 0), (1, -1), (-1, 1), (0, 1), (1, 1), (1, 0)]
        for dx, dy in toward:
            if True:
                flip = -1 if mode == "recv" else 1
                ok = jnp.bool_(True)
                if dx * flip == -1:
                    ok = jnp.logical_and(ok, ix > 0)
                if dx * flip == 1:
                    ok = jnp.logical_and(ok, ix < count_x - 1)
                if dy * flip == -1:
                    ok = jnp.logical_and(ok, iy > 0)
                if dy * flip == 1:
                    ok = jnp.logical_and(ok, iy < count_y - 1)
                sx = 0 if dx == -1 else 1
                sy = 0 if dy == -1 else 1
                rows = pl.ds(0, HALO) if dx == -1 else pl.ds(size_x - HALO, HALO)
                if dy == 0:
                    src, dst, base = rows_out.at[sx, lev], rows_in.at[sx, lev], sx
                elif dx == 0:
                    src, dst, base = packed.at[g], packed_in.at[g, sy], 2 + sy
                else:
                    src, dst = packed.at[g, rows, :], diag_in.at[g, sx, sy]
                    base = 4 + 2 * sx + sy

                def go(src=src, dst=dst, base=base, target=(z, ix + dx, iy + dy)):
                    copy = pltpu.make_async_remote_copy(
                        src_ref=src,
                        dst_ref=dst,
                        send_sem=local.at[8 * g + base],
                        recv_sem=halo_recv.at[8 * g + base],
                        device_id=target,
                        device_id_type=MESH,
                    )
                    if mode == "start":
                        copy.start()
                    elif mode == "send":
                        copy.wait_send()
                    else:
                        copy.wait_recv()

                pl.when(ok)(go)

    def halo_out(g):
        pack = jnp.zeros((size_x, size_y), f32)
        for l in groups[g]:
            if l != first:
                for c in range(n_pieces):
                    if pieces[c][0] == l:
                        settle(c, cur.at[l, pieces[c][1]])
            for f in range(4):
                rows_out[0, order.index(l), f] = cur[l, f, 0:HALO]
                rows_out[1, order.index(l), f] = cur[l, f, size_x - HALO :]
                k = f * levels + l
                moved = pltpu.roll(cur[l, f], (width * k + half) % size_y, 1)
                pack = jnp.where(lane // width == k, moved, pack)
        packed[g] = pack
        halo_jobs(g, "start")

    halo_out(0)

    @pl.when(inner)
    def _():
        for c in specs:
            select_near(c)
            sel_outer(c).start()
        for c in specs:
            sel_inner(c).start()

    @pl.when(outer)
    def _():
        arrived(first, 0, near)
        cur[first] = jnp.where(mine == z, chunk(first, z)[...], chunk(first, near)[...])

    @pl.when(inner)
    def _():
        a = chunk(first, cross_outer)[...]
        a = jnp.where(mine == cross_inner, chunk(first, cross_inner)[...], a)
        a = jnp.where(mine == near, chunk(first, near)[...], a)
        cur[first] = jnp.where(mine == z, chunk(first, z)[...], a)

    halo_out(1)

    ext_x = size_x + 2 * HALO
    ext_y = 2 * size_y
    rpos = lax.broadcasted_iota(jnp.int32, (ext_x, ext_y), 0)
    cpos = lax.broadcasted_iota(jnp.int32, (ext_x, ext_y), 1)
    gx_pos = ix * size_x + jnp.where(rpos < size_x + HALO, rpos, rpos - ext_x)
    gy_pos = iy * size_y + jnp.where(cpos < size_y + size_y // 2, cpos, cpos - ext_y)
    beside = slice(size_y, ext_y)
    above = slice(size_x, size_x + HALO)
    below = slice(size_x + HALO, ext_x)
    has_up = ix < count_x - 1
    has_down = ix > 0

    def inside(rows):
        xs, ys = gx_pos[rows, beside], gy_pos[rows, beside]
        return (xs >= 0) & (xs < full_x) & (ys >= 0) & (ys < full_y)

    in_main, in_up, in_down = inside(slice(0, size_x)), inside(above), inside(below)

    batch_of(4, rim_full, count_x - 1).wait_recv()
    rim = jnp.concatenate([rim_full[g] for g in range(count_x)], axis=0)
    rim_hi = rim.astype(jnp.bfloat16)
    rim_lo = (rim - rim_hi.astype(f32)).astype(jnp.bfloat16)
    both = jnp.dot(
        jnp.concatenate([rim_hi, rim_lo], axis=0), table[...], preferred_element_type=f32
    )
    n_rows = 4 * levels
    edge = both[0:n_rows] + both[n_rows:]
    sides[...] = edge
    for s in range(2):
        begin = 2 * full_y + s * full_x
        sides_t[s, HALO : HALO + full_x, :] = edge[:, begin : begin + full_x].T
        sides_t[s, 0:HALO, :] = jnp.zeros((HALO, n_rows), f32)
        sides_t[s, HALO + full_x :, :] = jnp.zeros((HALO, n_rows), f32)
    lane1 = lax.broadcasted_iota(jnp.int32, (n_rows, size_y), 1)

    def x_side(begin):
        own = sides[:, pl.ds(pl.multiple_of(begin + col_off, 128), size_y)]
        after = lax.rem(iy + 1, count_y) * size_y
        before = lax.rem(iy + count_y - 1, count_y) * size_y
        nxt_b = sides[:, pl.ds(pl.multiple_of(begin + after, 128), size_y)]
        prv_b = sides[:, pl.ds(pl.multiple_of(begin + before, 128), size_y)]
        return jnp.concatenate([own, jnp.where(lane1 < size_y // 2, nxt_b, prv_b)], axis=1)

    def y_side(s):
        body_rows = sides_t[s, pl.ds(pl.multiple_of(row_off + HALO, 8), size_x), :]
        above = sides_t[s, pl.ds(pl.multiple_of(row_off + HALO + size_x, 8), HALO), :]
        below = sides_t[s, pl.ds(row_off, HALO), :]
        return jnp.concatenate([body_rows, above, below], axis=0)

    west, east = x_side(0), x_side(full_y)
    south, north = y_side(0), y_side(1)
    if count_y > 1:
        column = jnp.where(iy == 0, south, north)

    lane2 = lax.broadcasted_iota(jnp.int32, (size_x + 2 * HALO, size_y), 1)
    take_next = lax.rem(lane2, width) >= half
    rains = {}
    thirds = []
    summed = jnp.zeros((size_x, levels * coarse_y), f32)

    def split(a):
        parts = []
        for _ in range(3):
            parts.append(a.astype(jnp.bfloat16))
            a = a - parts[-1].astype(f32)
        return parts

    for l in order:
        at = order.index(l)
        g = at // SPLIT
        if l == groups[g][0]:
            halo_jobs(g, "recv")
            nxt = jnp.concatenate([packed_in[g, 0], diag_in[g, 0, 0], diag_in[g, 1, 0]], axis=0)
            prv = jnp.concatenate([packed_in[g, 1], diag_in[g, 0, 1], diag_in[g, 1, 1]], axis=0)
            mixed = jnp.where(take_next, nxt, prv)

        def extended(f):
            k = f * levels + l
            left = jnp.concatenate([cur[l, f], rows_in[0, at, f], rows_in[1, at, f]], axis=0)
            right = pltpu.roll(mixed, (size_y - (width * k + half)) % size_y, 1)
            return jnp.concatenate([left, right], axis=1)

        def frame(f):
            k = f * levels + l
            if count_y > 1:
                side = jnp.broadcast_to(column[:, k : k + 1], (ext_x, size_y))
            else:
                at_south = gy_pos[:, beside] < 0
                side = jnp.where(at_south, south[:, k : k + 1], north[:, k : k + 1])
            eastern = jnp.broadcast_to(east[k : k + 1], (HALO, ext_y))
            western = jnp.broadcast_to(west[k : k + 1], (HALO, ext_y))
            up_v = jnp.where(has_up, side[above], eastern[:, beside])
            down_v = jnp.where(has_down, side[below], western[:, beside])

            def put(a):
                left = jnp.concatenate(
                    [
                        a[0:size_x, 0:size_y],
                        jnp.where(has_up, a[above, 0:size_y], eastern[:, 0:size_y]),
                        jnp.where(has_down, a[below, 0:size_y], western[:, 0:size_y]),
                    ],
                    axis=0,
                )
                right = jnp.concatenate(
                    [
                        jnp.where(in_main, a[0:size_x, beside], side[0:size_x]),
                        jnp.where(in_up, a[above, beside], up_v),
                        jnp.where(in_down, a[below, beside], down_v),
                    ],
                    axis=0,
                )
                return jnp.concatenate([left, right], axis=1)

            return put

        def up(a):
            return pltpu.roll(a, ext_x - 1, 0)

        def down(a):
            return pltpu.roll(a, 1, 0)

        def right_of(a):
            return pltpu.roll(a, ext_y - 1, 1)

        def left_of(a):
            return pltpu.roll(a, 1, 1)

        put_h, put_u, put_v, put_q = frame(0), frame(1), frame(2), frame(3)
        h, u, v, q = extended(0), extended(1), extended(2), extended(3)
        h = put_h(h)
        q = put_q(q)
        for substep in range(ACOUSTIC):
            u = u - acoustic_substep * (up(h) - down(h))
            v = v - acoustic_substep * (right_of(h) - left_of(h))
            u = put_u(u)
            v = put_v(v)
            h = h - acoustic_substep * ((up(u) - down(u)) + (right_of(v) - left_of(v)))
            h = put_h(h)
        flux = (
            jnp.maximum(u, 0.0) * (q - down(q)) + jnp.minimum(u, 0.0) * (up(q) - q)
        ) + (
            jnp.maximum(v, 0.0) * (q - left_of(q)) + jnp.minimum(v, 0.0) * (right_of(q) - q)
        )
        q = (q - drift_step * flux)[0:size_x, 0:size_y]
        fallen = cond_rate[l] * jnp.maximum(q - saturation[l], 0.0)
        q_new = q - fallen
        height_out[0, l] = h[0:size_x, 0:size_y]
        wind_out[0, 0, l] = u[0:size_x, 0:size_y]
        wind_out[0, 1, l] = v[0:size_x, 0:size_y]
        moisture_out[0, l] = q_new
        rains[l] = fallen
        thirds += split(q_new)
        if l == groups[g][-1]:
            span = spread[:, 3 * size_y * (at + 1 - len(groups[g])) : 3 * size_y * (at + 1)]
            summed = summed + lax.dot_general(
                jnp.concatenate(thirds, axis=1),
                span,
                (((1,), (1,)), ((), ())),
                preferred_element_type=f32,
            )
            thirds = []

    for n, third in enumerate(split(summed)):
        start = pl.multiple_of(n * full_x + row_off, 16)
        coarse_rows_buf[pl.ds(start, size_x), :] = third
    coarse_part[...] = jnp.dot(
        row_table3[...], coarse_rows_buf[...], preferred_element_type=f32
    )

    def crs_copy(other):
        px, py = other // count_y, other % count_y
        return pltpu.make_async_remote_copy(
            src_ref=coarse_part,
            dst_ref=coarse_in.at[here],
            send_sem=batch.at[6],
            recv_sem=batch.at[7],
            device_id=(z, px, py),
            device_id_type=MESH,
        )

    for other in range(plane):
        pl.when(here != other)(crs_copy(other).start)
    rain = rains[0]
    for l in range(1, levels):
        rain = rain + rains[l]
    rain_out[0] = rain

    for half_at, c in enumerate(specs):
        settle(c, coeffs_out.at[0, pl.ds(2 * half_at, 2)])

    batch_of(6, coarse_in, plane - 1).wait_recv()
    total = coarse_part[...]
    for step in range(1, plane):
        other, _, _ = plane_peer(step)
        total = total + coarse_in[other]
    total = total / (row_count * col_count)
    for l in range(levels):
        coarse_out[0, l] = total[:, l * coarse_y : (l + 1) * coarse_y]

    for g in range(2):
        halo_jobs(g, "send")
    batch_of(0, rim_in, plane - 1).wait_send()
    batch_of(2, rim_z, members - 1).wait_send()
    batch_of(4, rim_full, count_x - 1).wait_send()
    batch_of(6, coarse_in, plane - 1).wait_send()

    def sent(n, ref, count):
        many = ref.at[pl.ds(0, count)]
        pltpu.make_async_remote_copy(
            src_ref=many,
            dst_ref=many,
            send_sem=mem_send.at[n],
            recv_sem=mem_recv.at[0],
            device_id=(near, ix, iy),
            device_id_type=MESH,
        ).wait_send()

    @pl.when(outer)
    def _():
        sent(0, st, levels + 1)
        sent(1, cf, 2)

    @pl.when(inner)
    def _():
        sent(0, st, 3 * levels - 1)
        sent(1, cf, 6)


def write_out(*refs):
    sems = refs[12]
    copies = [pltpu.make_async_copy(refs[n], refs[6 + n], sems.at[n]) for n in range(6)]
    for copy in copies:
        copy.start()
    for copy in copies:
        copy.wait()


def body(
    sizes,
    height,
    wind,
    moisture,
    coeffs,
    damping,
    vmix,
    basis,
    edge_source,
    row_cell,
    col_cell,
    cond_rate,
    saturation,
    ancestry,
):
    members, count_x, count_y = sizes
    plane = count_x * count_y
    _, levels, size_x, size_y = height.shape
    local_k = coeffs.shape[3]
    rim_points = basis.shape[1]
    full_x = row_cell.shape[0]
    full_y = col_cell.shape[0]
    n_edge = edge_source.shape[0]
    coarse_x, coarse_y = full_x // RATIO, full_y // RATIO
    share = 4 * levels // count_x
    rows = 4 * levels
    f32 = jnp.float32
    vmem = pl.BlockSpec(memory_space=pltpu.VMEM)
    dma = pltpu.SemaphoreType.DMA
    coarse_chunk = (coarse_x, levels * coarse_y)
    operands = (
        height,
        wind,
        moisture,
        coeffs,
        damping.reshape(1, -1),
        vmix,
        basis,
        edge_source,
        row_cell.reshape(1, -1),
        col_cell.reshape(1, -1),
        cond_rate,
        saturation,
        ancestry,
    )
    chunks = levels + 3
    scratch = [
        *[pltpu.VMEM(a.shape, a.dtype) for a in operands[3:10]],
        *[pltpu.SMEM(a.shape, a.dtype) for a in operands[10:]],
        pltpu.VMEM((members * levels, 4, size_x, size_y), f32),
        pltpu.VMEM((members * 2, 2, levels, local_k), f32),
        pltpu.VMEM((2, levels, 4, size_x, size_y), f32),
        pltpu.VMEM((2, 2, 2, levels, local_k), f32),
        pltpu.VMEM((4, size_x, size_y), f32),
        pltpu.VMEM((levels, 4, size_x, size_y), f32),
        pltpu.VMEM((2, levels, 4, HALO, size_y), f32),
        pltpu.VMEM((2, levels, 4, HALO, size_y), f32),
        pltpu.VMEM((2, size_x, size_y), f32),
        pltpu.VMEM((2, 2, size_x, size_y), f32),
        pltpu.VMEM((2, 2, 2, HALO, size_y), f32),
        pltpu.VMEM((count_x, share, rim_points), f32),
        pltpu.VMEM((plane, share, rim_points), f32),
        pltpu.VMEM((members, share, rim_points), f32),
        pltpu.VMEM((count_x, share, rim_points), f32),
        pltpu.VMEM((rim_points, n_edge), jnp.bfloat16),
        pltpu.VMEM((rows, n_edge), f32),
        pltpu.VMEM((2, full_x + 2 * HALO, rows), f32),
        pltpu.VMEM((levels * coarse_y, 3 * levels * size_y), jnp.bfloat16),
        pltpu.VMEM((coarse_x, 3 * full_x), jnp.bfloat16),
        pltpu.VMEM((3 * full_x, levels * coarse_y), jnp.bfloat16),
        pltpu.VMEM(coarse_chunk, f32),
        pltpu.VMEM((plane, *coarse_chunk), f32),
        dma((16,)),
        dma((8,)),
        dma((2,)),
        dma((1 + 2 * chunks,)),
        dma((16,)),
        pltpu.SemaphoreType.REGULAR((max(plane.bit_length() - 2, 2),)),
    ]
    outs = (
        pltpu.VMEM(height.shape, f32),
        pltpu.VMEM(wind.shape, f32),
        pltpu.VMEM(moisture.shape, f32),
        pltpu.VMEM((1, size_x, size_y), f32),
        pltpu.VMEM((1, levels, coarse_x, coarse_y), f32),
        pltpu.VMEM(coeffs.shape, f32),
    )
    results = pl.pallas_call(
        functools.partial(kernel, sizes),
        out_shape=outs,
        in_specs=[pl.BlockSpec(memory_space=pltpu.HBM)] * 13,
        out_specs=(vmem,) * 6,
        scratch_shapes=scratch,
        compiler_params=pltpu.CompilerParams(
            collective_id=0, has_side_effects=True, vmem_limit_bytes=36 * 1024 * 1024
        ),
    )(*[pltpu.with_memory_space_constraint(a, pltpu.HBM) for a in operands])
    return pl.pallas_call(
        write_out,
        out_shape=tuple(jax.ShapeDtypeStruct(r.shape, f32) for r in results),
        in_specs=[vmem] * 6,
        out_specs=(pl.BlockSpec(memory_space=pl.ANY),) * 6,
        scratch_shapes=[dma((6,))],
        compiler_params=pltpu.CompilerParams(vmem_limit_bytes=8 * 1024 * 1024),
    )(*results)


def solution(mesh):
    sizes = (mesh.shape["mem"], mesh.shape["gx"], mesh.shape["gy"])
    in_specs = (
        P("mem", None, "gx", "gy"),
        P("mem", None, None, "gx", "gy"),
        P("mem", None, "gx", "gy"),
        P("mem", None, None, ("gx", "gy")),
        P(("gx", "gy")),
        P(),
        P(("gx", "gy"), None),
        P(),
        P(),
        P(),
        P(),
        P(),
        P(),
    )
    out_specs = (
        P("mem", None, "gx", "gy"),
        P("mem", None, None, "gx", "gy"),
        P("mem", None, "gx", "gy"),
        P("mem", "gx", "gy"),
        P("mem", None, None, None),
        P("mem", None, None, ("gx", "gy")),
    )
    return jax.shard_map(
        functools.partial(body, sizes),
        mesh=mesh,
        in_specs=in_specs,
        out_specs=out_specs,
        check_vma=False,
    )
```

```python
import functools

import jax
import jax.numpy as jnp
from jax import lax
from jax.experimental import pallas as pl
from jax.experimental.pallas import tpu as pltpu
from jax.sharding import PartitionSpec as P

RATIO = 8
ACOUSTIC = 2
HALO = 8
SPLIT = 2

acoustic_substep = 0.2
drift_step = 0.4

MESH = pl.DeviceIdType.MESH


def kernel(
    sizes,
    height,
    wind,
    moisture,
    coeffs_hbm,
    damping_hbm,
    vmix_hbm,
    basis_hbm,
    edge_source_hbm,
    row_cell_hbm,
    col_cell_hbm,
    cond_rate_hbm,
    saturation_hbm,
    ancestry_hbm,
    height_out,
    wind_out,
    moisture_out,
    rain_out,
    coarse_out,
    coeffs_out,
    coeffs,
    damping,
    vmix,
    basis,
    edge_source,
    row_cell,
    col_cell,
    cond_rate,
    saturation,
    ancestry,
    st,
    cf,
    st_sel,
    cf_sel,
    st_relay,
    cur,
    rows_out,
    rows_in,
    packed,
    packed_in,
    diag_in,
    rim_part,
    rim_in,
    rim_z,
    rim_full,
    table,
    sides,
    sides_t,
    spread,
    row_table3,
    coarse_rows_buf,
    coarse_part,
    coarse_in,
    halo_recv,
    batch,
    mem_send,
    mem_recv,
    local,
    rounds,
):
    members, count_x, count_y = sizes
    plane = count_x * count_y
    levels = cur.shape[0]
    size_x = st.shape[2]
    size_y = st.shape[3]
    full_x = row_cell.shape[1]
    full_y = col_cell.shape[1]
    rim_points = basis.shape[1]
    coarse_x = coarse_out.shape[2]
    coarse_y = coarse_out.shape[3]
    share = rim_part.shape[1]
    f32 = jnp.float32

    z = lax.axis_index("mem")
    ix = lax.axis_index("gx")
    iy = lax.axis_index("gy")
    here = ix * count_y + iy
    low_side = z < 2
    inner = jnp.logical_and(z > 0, z < members - 1)
    outer = jnp.logical_not(inner)
    near = jnp.where(low_side, 1 - z, 5 - z)
    cross_inner = jnp.where(low_side, 2, 1)
    cross_outer = jnp.where(low_side, 3, 0)

    def plane_peer(step):
        other = lax.rem(here + step, plane)
        return other, other // count_y, lax.rem(other, count_y)

    own_slots = pl.ds(z * levels, levels)
    loads = [
        (height.at[0], st.at[own_slots, 0]),
        (wind.at[0, 0], st.at[own_slots, 1]),
        (wind.at[0, 1], st.at[own_slots, 2]),
        (moisture.at[0], st.at[own_slots, 3]),
        (coeffs_hbm, coeffs),
        (damping_hbm, damping),
        (vmix_hbm, vmix),
        (basis_hbm, basis),
        (edge_source_hbm, edge_source),
        (row_cell_hbm, row_cell),
        (col_cell_hbm, col_cell),
        (cond_rate_hbm, cond_rate),
        (saturation_hbm, saturation),
        (ancestry_hbm, ancestry),
    ]
    copies = [pltpu.make_async_copy(a, b, local.at[n]) for n, (a, b) in enumerate(loads)]
    for copy in copies:
        copy.start()

    def ready(*which):
        for n in which:
            copies[n].wait()

    if plane & (plane - 1):
        steps = [lax.rem(here + step, plane) for step in range(1, plane)]
        n_rounds = 2
    else:
        n_dims = plane.bit_length() - 1
        n_rounds = max(n_dims - 1, 2)
        steps = []
        for k in range(n_dims):
            bit = lax.rem(here // 2**k, 2)
            steps.append(here + 2**k * (1 - 2 * bit))

    def greet(sem, n):
        for other in steps:
            pl.semaphore_signal(
                sem,
                inc=1,
                device_id=(z, other // count_y, lax.rem(other, count_y)),
                device_id_type=MESH,
            )
        pl.semaphore_signal(sem, inc=1, device_id=(near, ix, iy), device_id_type=MESH)

        @pl.when(inner)
        def _():
            for other in (cross_inner, cross_outer)[:n]:
                pl.semaphore_signal(
                    sem, inc=1, device_id=(other, ix, iy), device_id_type=MESH
                )

    barrier = pltpu.get_barrier_semaphore()
    greet(barrier, 2)

    ready(0, 1, 2, 3)

    pl.semaphore_wait(barrier, len(steps) + 2)
    greet(rounds.at[0], 1)

    pieces = [(0, pl.ds(0, 4)), (1, pl.ds(0, 2)), (1, pl.ds(2, 2))]
    pieces += [(l, pl.ds(0, 4)) for l in range(2, levels)]
    n_pieces = len(pieces)

    def chunk(c, slot):
        if c >= n_pieces:
            return cf.at[slot * 2 + c - n_pieces]
        return st.at[slot * levels + pieces[c][0], pieces[c][1]]

    def chosen(c, way):
        if c >= n_pieces:
            return cf_sel.at[way, c - n_pieces]
        return st_sel.at[way, pieces[c][0], pieces[c][1]]

    def z_copy(c, kind, src, slot, target):
        return pltpu.make_async_remote_copy(
            src_ref=src,
            dst_ref=chunk(c, slot),
            send_sem=mem_send.at[0 if c < n_pieces else 1],
            recv_sem=mem_recv.at[kind if c == 0 else 1 + 2 * c + kind],
            device_id=(target, ix, iy),
            device_id_type=MESH,
        )

    def own_near(c):
        return z_copy(c, 0, chunk(c, z), z, near)

    def own_cross(c):
        return z_copy(c, jnp.where(outer, 2, 1), chunk(c, z), z, cross_inner)

    def sel_inner(c):
        return z_copy(c, 1, chosen(c, 0), z, cross_inner)

    def sel_outer(c):
        return z_copy(c, 1, chosen(c, 1), z, cross_outer)

    def relay_near(c):
        return z_copy(c, 0, st_relay, z, near)

    def arrived(c, kind, slot):
        z_copy(c, kind, chunk(c, slot), slot, near).wait_recv()

    first, rest = 0, list(range(1, n_pieces))
    specs = [n_pieces, n_pieces + 1]
    lead, later = rest[:2], rest[2:]

    @pl.when(inner)
    def _():
        own_cross(first).start()
        for c in rest:
            own_near(c).start()

    @pl.when(outer)
    def _():
        for c in lead:
            own_near(c).start()
        own_cross(first).start()
        for c in later:
            own_near(c).start()

    ready(4, 5, 6)
    new_fields = []
    for f in range(4):
        c = coeffs[0, f]
        acc = vmix[:, 0:1] * c[0:1]
        for j in range(1, levels):
            acc = acc + vmix[:, j : j + 1] * c[j : j + 1]
        new_fields.append(acc * damping[...])
    for f in range(4):
        cf[2 * z + f // 2, f % 2] = new_fields[f]
    pl.semaphore_wait(rounds.at[0], len(steps) + jnp.where(inner, 2, 1))
    for k in range(1, n_rounds):
        greet(rounds.at[k], 0)
        if k < n_rounds - 1:
            pl.semaphore_wait(rounds.at[k], len(steps) + 1)
    low = jnp.concatenate(new_fields, axis=0).astype(jnp.bfloat16)
    ready(7)
    part = jnp.dot(low, basis[...], preferred_element_type=f32)
    for g in range(count_x):
        rim_part[g] = part[g * share : (g + 1) * share]

    def rim_copy(step):
        _, px, py = plane_peer(step)
        return pltpu.make_async_remote_copy(
            src_ref=rim_part.at[px],
            dst_ref=rim_in.at[here],
            send_sem=batch.at[0],
            recv_sem=batch.at[1],
            device_id=(z, px, py),
            device_id_type=MESH,
        )

    pl.semaphore_wait(rounds.at[n_rounds - 1], len(steps) + 1)
    for step in range(1, plane):
        rim_copy(step).start()

    ready(8, 9, 10, 11, 12, 13)
    mine = ancestry[z]

    def select_near(c):
        arrived(c, 0, near)
        for way, target in ((0, cross_inner), (1, cross_outer)):
            take_own = ancestry[target] != near
            chosen(c, way)[...] = jnp.where(take_own, chunk(c, z)[...], chunk(c, near)[...])

    n_edge = edge_source.shape[0]
    table[...] = (
        (lax.broadcasted_iota(jnp.int32, (rim_points, n_edge), 0)
         == edge_source[...].reshape(1, n_edge))
        .astype(f32)
        .astype(jnp.bfloat16)
    )
    row_table = (
        lax.broadcasted_iota(jnp.int32, (coarse_x, full_x), 0) == row_cell[...]
    ).astype(f32)
    row_count = jnp.sum(row_table, axis=1, keepdims=True)
    wide = lax.rem(
        lax.broadcasted_iota(jnp.int32, (levels * coarse_y, full_y), 0), coarse_y
    )
    col_table = (wide == col_cell[...]).astype(f32)
    col_count = lax.dot_general(
        jnp.ones((8, full_y), f32),
        col_table,
        (((1,), (1,)), ((), ())),
        preferred_element_type=f32,
    )[0:1]
    col_off = pl.multiple_of(iy * size_y, 128)
    row_off = pl.multiple_of(ix * size_x, 8)
    cells_here = col_cell[:, pl.ds(col_off, size_y)]
    wide_here = lax.broadcasted_iota(jnp.int32, (levels * coarse_y, size_y), 0)
    coarse_rows_buf[...] = jnp.zeros_like(coarse_rows_buf)
    for m in range(3):
        row_table3[:, m * full_x : (m + 1) * full_x] = row_table.astype(jnp.bfloat16)

    @pl.when(inner)
    def _():
        for c in lead:
            select_near(c)
            sel_outer(c).start()
            sel_inner(c).start()

    def batch_of(n, ref, count):
        many = ref.at[pl.ds(0, count)]
        return pltpu.make_async_remote_copy(
            src_ref=many,
            dst_ref=many,
            send_sem=batch.at[n],
            recv_sem=batch.at[n + 1],
            device_id=(near, ix, iy),
            device_id_type=MESH,
        )

    batch_of(0, rim_in, plane - 1).wait_recv()
    total = rim_part[ix]
    for step in range(1, plane):
        other, _, _ = plane_peer(step)
        total = total + rim_in[other]
    rim_z[z] = total

    def rimz_copy(step, source):
        return pltpu.make_async_remote_copy(
            src_ref=rim_z.at[source],
            dst_ref=rim_z.at[source],
            send_sem=batch.at[2],
            recv_sem=batch.at[3],
            device_id=(lax.rem(z + step, members), ix, iy),
            device_id_type=MESH,
        )

    for step in range(1, members):
        rimz_copy(step, z).start()

    @pl.when(outer)
    def _():
        for c in [first] + specs:
            own_near(c).start()

    @pl.when(inner)
    def _():
        arrived(first, 1, cross_inner)
        arrived(first, 2, cross_outer)
        want = ancestry[near]
        a = chunk(first, z)[...]
        a = jnp.where(want == cross_inner, chunk(first, cross_inner)[...], a)
        st_relay[...] = jnp.where(want == cross_outer, chunk(first, cross_outer)[...], a)
        relay_near(first).start()
        for c in later:
            select_near(c)
            sel_outer(c).start()
        for c in later:
            sel_inner(c).start()

    batch_of(2, rim_z, members - 1).wait_recv()
    share_sel = rim_z[z]
    for step in range(1, members):
        source = lax.rem(z + step, members)
        share_sel = jnp.where(mine == source, rim_z[source], share_sel)
    rim_full[ix] = share_sel

    def rimg_copy(step, source):
        return pltpu.make_async_remote_copy(
            src_ref=rim_full.at[source],
            dst_ref=rim_full.at[source],
            send_sem=batch.at[4],
            recv_sem=batch.at[5],
            device_id=(z, lax.rem(ix + step, count_x), iy),
            device_id_type=MESH,
        )

    for step in range(1, count_x):
        rimg_copy(step, ix).start()

    @pl.when(inner)
    def _():
        arrived(first, 0, near)
        for c in specs:
            own_near(c).start()

    lane = lax.broadcasted_iota(jnp.int32, (size_x, size_y), 1)
    width = size_y // (4 * levels)
    half = width // 2

    def settle(c, ref):
        arrived(c, 1, cross_inner)

        @pl.when(outer)
        def _():
            arrived(c, 0, near)

        a = jnp.where(mine == z, chunk(c, z)[...], chunk(c, cross_inner)[...])
        ref[...] = jnp.where(mine == near, chunk(c, near)[...], a)

    order = list(range(1, levels - 1)) + [first, levels - 1]
    groups = [order[:SPLIT], order[SPLIT:]]
    for n, l in enumerate(order):
        hit = ((wide_here - l * coarse_y) == cells_here).astype(f32).astype(jnp.bfloat16)
        for m in range(3):
            spread[:, (3 * n + m) * size_y : (3 * n + m + 1) * size_y] = hit

    def halo_jobs(g, mode):
        lev = pl.ds(SPLIT * g, len(groups[g]))
        toward = [(-1, -1), (0, -1), (-1, 0), (1, -1), (-1, 1), (0, 1), (1, 1), (1, 0)]
        for dx, dy in toward:
            if True:
                flip = -1 if mode == "recv" else 1
                ok = jnp.bool_(True)
                if dx * flip == -1:
                    ok = jnp.logical_and(ok, ix > 0)
                if dx * flip == 1:
                    ok = jnp.logical_and(ok, ix < count_x - 1)
                if dy * flip == -1:
                    ok = jnp.logical_and(ok, iy > 0)
                if dy * flip == 1:
                    ok = jnp.logical_and(ok, iy < count_y - 1)
                sx = 0 if dx == -1 else 1
                sy = 0 if dy == -1 else 1
                rows = pl.ds(0, HALO) if dx == -1 else pl.ds(size_x // 2 - HALO, HALO)
                if dy == 0:
                    src, dst, base = rows_out.at[sx, lev], rows_in.at[sx, lev], sx
                elif dx == 0:
                    src, dst, base = packed.at[g], packed_in.at[g, sy], 2 + sy
                else:
                    src, dst = packed.at[g, rows, :], diag_in.at[g, sx, sy]
                    base = 4 + 2 * sx + sy

                def go(src=src, dst=dst, base=base, target=(z, ix + dx, iy + dy)):
                    copy = pltpu.make_async_remote_copy(
                        src_ref=src,
                        dst_ref=dst,
                        send_sem=local.at[8 * g + base],
                        recv_sem=halo_recv.at[8 * g + base],
                        device_id=target,
                        device_id_type=MESH,
                    )
                    if mode == "start":
                        copy.start()
                    elif mode == "send":
                        copy.wait_send()
                    else:
                        copy.wait_recv()

                pl.when(ok)(go)

    fold = size_x // 2

    def halo_out(g):
        pack = jnp.zeros((size_x, size_y), f32)
        for l in groups[g]:
            if l != first:
                for c in range(n_pieces):
                    if pieces[c][0] == l:
                        settle(c, cur.at[l, pieces[c][1]])
            for f in range(4):
                rows_out[0, order.index(l), f] = cur[l, f, 0:HALO]
                rows_out[1, order.index(l), f] = cur[l, f, size_x - HALO :]
                k = f * len(groups[g]) + groups[g].index(l)
                moved = pltpu.roll(cur[l, f], (width * k + half) % size_y, 1)
                pack = jnp.where(lane // width == k, moved, pack)
        below_half = pltpu.roll(pack[fold:], size_y // 2, 1)
        packed[g] = jnp.where(lane[:fold] < size_y // 2, pack[:fold], below_half)
        halo_jobs(g, "start")

    halo_out(0)

    @pl.when(inner)
    def _():
        for c in specs:
            select_near(c)
            sel_outer(c).start()
        for c in specs:
            sel_inner(c).start()

    @pl.when(outer)
    def _():
        arrived(first, 0, near)
        cur[first] = jnp.where(mine == z, chunk(first, z)[...], chunk(first, near)[...])

    @pl.when(inner)
    def _():
        a = chunk(first, cross_outer)[...]
        a = jnp.where(mine == cross_inner, chunk(first, cross_inner)[...], a)
        a = jnp.where(mine == near, chunk(first, near)[...], a)
        cur[first] = jnp.where(mine == z, chunk(first, z)[...], a)

    halo_out(1)

    ext_x = size_x + 2 * HALO
    ext_y = 2 * size_y
    rpos = lax.broadcasted_iota(jnp.int32, (ext_x, ext_y), 0)
    cpos = lax.broadcasted_iota(jnp.int32, (ext_x, ext_y), 1)
    gx_pos = ix * size_x + jnp.where(rpos < size_x + HALO, rpos, rpos - ext_x)
    gy_pos = iy * size_y + jnp.where(cpos < size_y + size_y // 2, cpos, cpos - ext_y)
    beside = slice(size_y, ext_y)
    above = slice(size_x, size_x + HALO)
    below = slice(size_x + HALO, ext_x)
    has_up = ix < count_x - 1
    has_down = ix > 0

    def inside(rows):
        xs, ys = gx_pos[rows, beside], gy_pos[rows, beside]
        return (xs >= 0) & (xs < full_x) & (ys >= 0) & (ys < full_y)

    in_main, in_up, in_down = inside(slice(0, size_x)), inside(above), inside(below)

    batch_of(4, rim_full, count_x - 1).wait_recv()
    rim = jnp.concatenate([rim_full[g] for g in range(count_x)], axis=0)
    rim_hi = rim.astype(jnp.bfloat16)
    rim_lo = (rim - rim_hi.astype(f32)).astype(jnp.bfloat16)
    both = jnp.dot(
        jnp.concatenate([rim_hi, rim_lo], axis=0), table[...], preferred_element_type=f32
    )
    n_rows = 4 * levels
    edge = both[0:n_rows] + both[n_rows:]
    sides[...] = edge
    for s in range(2):
        begin = 2 * full_y + s * full_x
        sides_t[s, HALO : HALO + full_x, :] = edge[:, begin : begin + full_x].T
        sides_t[s, 0:HALO, :] = jnp.zeros((HALO, n_rows), f32)
        sides_t[s, HALO + full_x :, :] = jnp.zeros((HALO, n_rows), f32)
    lane1 = lax.broadcasted_iota(jnp.int32, (n_rows, size_y), 1)

    def x_side(begin):
        own = sides[:, pl.ds(pl.multiple_of(begin + col_off, 128), size_y)]
        after = lax.rem(iy + 1, count_y) * size_y
        before = lax.rem(iy + count_y - 1, count_y) * size_y
        nxt_b = sides[:, pl.ds(pl.multiple_of(begin + after, 128), size_y)]
        prv_b = sides[:, pl.ds(pl.multiple_of(begin + before, 128), size_y)]
        return jnp.concatenate([own, jnp.where(lane1 < size_y // 2, nxt_b, prv_b)], axis=1)

    def y_side(s):
        body_rows = sides_t[s, pl.ds(pl.multiple_of(row_off + HALO, 8), size_x), :]
        above = sides_t[s, pl.ds(pl.multiple_of(row_off + HALO + size_x, 8), HALO), :]
        below = sides_t[s, pl.ds(row_off, HALO), :]
        return jnp.concatenate([body_rows, above, below], axis=0)

    west, east = x_side(0), x_side(full_y)
    south, north = y_side(0), y_side(1)
    if count_y > 1:
        column = jnp.where(iy == 0, south, north)

    lane2 = lax.broadcasted_iota(jnp.int32, (size_x + 2 * HALO, size_y), 1)
    take_next = lax.rem(lane2, width) >= half
    rains = {}
    thirds = []
    summed = jnp.zeros((size_x, levels * coarse_y), f32)

    def split(a):
        parts = []
        for _ in range(3):
            parts.append(a.astype(jnp.bfloat16))
            a = a - parts[-1].astype(f32)
        return parts

    for l in order:
        at = order.index(l)
        g = at // SPLIT
        if l == groups[g][0]:
            halo_jobs(g, "recv")


            def unfold(way):
                part = packed_in[g, way]
                turned = pltpu.roll(part, size_y // 2, 1)
                corner = pltpu.roll(diag_in[g, 1, way], size_y // 2, 1)
                return jnp.concatenate([part, turned, diag_in[g, 0, way], corner], axis=0)

            mixed = jnp.where(take_next, unfold(0), unfold(1))

        def extended(f):
            k = f * len(groups[g]) + groups[g].index(l)
            left = jnp.concatenate([cur[l, f], rows_in[0, at, f], rows_in[1, at, f]], axis=0)
            right = pltpu.roll(mixed, (size_y - (width * k + half)) % size_y, 1)
            return jnp.concatenate([left, right], axis=1)

        def frame(f):
            k = f * levels + l
            if count_y > 1:
                side = jnp.broadcast_to(column[:, k : k + 1], (ext_x, size_y))
            else:
                at_south = gy_pos[:, beside] < 0
                side = jnp.where(at_south, south[:, k : k + 1], north[:, k : k + 1])
            eastern = jnp.broadcast_to(east[k : k + 1], (HALO, ext_y))
            western = jnp.broadcast_to(west[k : k + 1], (HALO, ext_y))
            up_v = jnp.where(has_up, side[above], eastern[:, beside])
            down_v = jnp.where(has_down, side[below], western[:, beside])

            def put(a):
                left = jnp.concatenate(
                    [
                        a[0:size_x, 0:size_y],
                        jnp.where(has_up, a[above, 0:size_y], eastern[:, 0:size_y]),
                        jnp.where(has_down, a[below, 0:size_y], western[:, 0:size_y]),
                    ],
                    axis=0,
                )
                right = jnp.concatenate(
                    [
                        jnp.where(in_main, a[0:size_x, beside], side[0:size_x]),
                        jnp.where(in_up, a[above, beside], up_v),
                        jnp.where(in_down, a[below, beside], down_v),
                    ],
                    axis=0,
                )
                return jnp.concatenate([left, right], axis=1)

            return put

        def up(a):
            return pltpu.roll(a, ext_x - 1, 0)

        def down(a):
            return pltpu.roll(a, 1, 0)

        def right_of(a):
            return pltpu.roll(a, ext_y - 1, 1)

        def left_of(a):
            return pltpu.roll(a, 1, 1)

        put_h, put_u, put_v, put_q = frame(0), frame(1), frame(2), frame(3)
        h, u, v, q = extended(0), extended(1), extended(2), extended(3)
        h = put_h(h)
        q = put_q(q)
        for substep in range(ACOUSTIC):
            u = u - acoustic_substep * (up(h) - down(h))
            v = v - acoustic_substep * (right_of(h) - left_of(h))
            u = put_u(u)
            v = put_v(v)
            h = h - acoustic_substep * ((up(u) - down(u)) + (right_of(v) - left_of(v)))
            h = put_h(h)
        flux = (
            jnp.maximum(u, 0.0) * (q - down(q)) + jnp.minimum(u, 0.0) * (up(q) - q)
        ) + (
            jnp.maximum(v, 0.0) * (q - left_of(q)) + jnp.minimum(v, 0.0) * (right_of(q) - q)
        )
        q = (q - drift_step * flux)[0:size_x, 0:size_y]
        fallen = cond_rate[l] * jnp.maximum(q - saturation[l], 0.0)
        q_new = q - fallen
        height_out[0, l] = h[0:size_x, 0:size_y]
        wind_out[0, 0, l] = u[0:size_x, 0:size_y]
        wind_out[0, 1, l] = v[0:size_x, 0:size_y]
        moisture_out[0, l] = q_new
        rains[l] = fallen
        thirds += split(q_new)
        if l == groups[g][-1]:
            span = spread[:, 3 * size_y * (at + 1 - len(groups[g])) : 3 * size_y * (at + 1)]
            summed = summed + lax.dot_general(
                jnp.concatenate(thirds, axis=1),
                span,
                (((1,), (1,)), ((), ())),
                preferred_element_type=f32,
            )
            thirds = []

    for n, third in enumerate(split(summed)):
        start = pl.multiple_of(n * full_x + row_off, 16)
        coarse_rows_buf[pl.ds(start, size_x), :] = third
    coarse_part[...] = jnp.dot(
        row_table3[...], coarse_rows_buf[...], preferred_element_type=f32
    )

    def crs_copy(other):
        px, py = other // count_y, other % count_y
        return pltpu.make_async_remote_copy(
            src_ref=coarse_part,
            dst_ref=coarse_in.at[here],
            send_sem=batch.at[6],
            recv_sem=batch.at[7],
            device_id=(z, px, py),
            device_id_type=MESH,
        )

    for other in range(plane):
        pl.when(here != other)(crs_copy(other).start)
    rain = rains[0]
    for l in range(1, levels):
        rain = rain + rains[l]
    rain_out[0] = rain

    for half_at, c in enumerate(specs):
        settle(c, coeffs_out.at[0, pl.ds(2 * half_at, 2)])

    for g in range(2):
        halo_jobs(g, "send")
    batch_of(0, rim_in, plane - 1).wait_send()
    batch_of(2, rim_z, members - 1).wait_send()
    batch_of(4, rim_full, count_x - 1).wait_send()

    def sent(n, ref, count):
        many = ref.at[pl.ds(0, count)]
        pltpu.make_async_remote_copy(
            src_ref=many,
            dst_ref=many,
            send_sem=mem_send.at[n],
            recv_sem=mem_recv.at[0],
            device_id=(near, ix, iy),
            device_id_type=MESH,
        ).wait_send()

    @pl.when(outer)
    def _():
        sent(0, st, levels + 1)
        sent(1, cf, 2)

    @pl.when(inner)
    def _():
        sent(0, st, 3 * levels - 1)
        sent(1, cf, 6)

    batch_of(6, coarse_in, plane - 1).wait_recv()
    total = coarse_part[...]
    for step in range(1, plane):
        other, _, _ = plane_peer(step)
        total = total + coarse_in[other]
    total = total / (row_count * col_count)
    for l in range(levels):
        coarse_out[0, l] = total[:, l * coarse_y : (l + 1) * coarse_y]

    batch_of(6, coarse_in, plane - 1).wait_send()


def write_out(*refs):
    sems = refs[12]
    copies = [pltpu.make_async_copy(refs[n], refs[6 + n], sems.at[n]) for n in range(6)]
    for copy in copies:
        copy.start()
    for copy in copies:
        copy.wait()


def body(
    sizes,
    height,
    wind,
    moisture,
    coeffs,
    damping,
    vmix,
    basis,
    edge_source,
    row_cell,
    col_cell,
    cond_rate,
    saturation,
    ancestry,
):
    members, count_x, count_y = sizes
    plane = count_x * count_y
    _, levels, size_x, size_y = height.shape
    local_k = coeffs.shape[3]
    rim_points = basis.shape[1]
    full_x = row_cell.shape[0]
    full_y = col_cell.shape[0]
    n_edge = edge_source.shape[0]
    coarse_x, coarse_y = full_x // RATIO, full_y // RATIO
    share = 4 * levels // count_x
    rows = 4 * levels
    f32 = jnp.float32
    vmem = pl.BlockSpec(memory_space=pltpu.VMEM)
    dma = pltpu.SemaphoreType.DMA
    coarse_chunk = (coarse_x, levels * coarse_y)
    operands = (
        height,
        wind,
        moisture,
        coeffs,
        damping.reshape(1, -1),
        vmix,
        basis,
        edge_source,
        row_cell.reshape(1, -1),
        col_cell.reshape(1, -1),
        cond_rate,
        saturation,
        ancestry,
    )
    chunks = levels + 3
    scratch = [
        *[pltpu.VMEM(a.shape, a.dtype) for a in operands[3:10]],
        *[pltpu.SMEM(a.shape, a.dtype) for a in operands[10:]],
        pltpu.VMEM((members * levels, 4, size_x, size_y), f32),
        pltpu.VMEM((members * 2, 2, levels, local_k), f32),
        pltpu.VMEM((2, levels, 4, size_x, size_y), f32),
        pltpu.VMEM((2, 2, 2, levels, local_k), f32),
        pltpu.VMEM((4, size_x, size_y), f32),
        pltpu.VMEM((levels, 4, size_x, size_y), f32),
        pltpu.VMEM((2, levels, 4, HALO, size_y), f32),
        pltpu.VMEM((2, levels, 4, HALO, size_y), f32),
        pltpu.VMEM((2, size_x // 2, size_y), f32),
        pltpu.VMEM((2, 2, size_x // 2, size_y), f32),
        pltpu.VMEM((2, 2, 2, HALO, size_y), f32),
        pltpu.VMEM((count_x, share, rim_points), f32),
        pltpu.VMEM((plane, share, rim_points), f32),
        pltpu.VMEM((members, share, rim_points), f32),
        pltpu.VMEM((count_x, share, rim_points), f32),
        pltpu.VMEM((rim_points, n_edge), jnp.bfloat16),
        pltpu.VMEM((rows, n_edge), f32),
        pltpu.VMEM((2, full_x + 2 * HALO, rows), f32),
        pltpu.VMEM((levels * coarse_y, 3 * levels * size_y), jnp.bfloat16),
        pltpu.VMEM((coarse_x, 3 * full_x), jnp.bfloat16),
        pltpu.VMEM((3 * full_x, levels * coarse_y), jnp.bfloat16),
        pltpu.VMEM(coarse_chunk, f32),
        pltpu.VMEM((plane, *coarse_chunk), f32),
        dma((16,)),
        dma((8,)),
        dma((2,)),
        dma((1 + 2 * chunks,)),
        dma((16,)),
        pltpu.SemaphoreType.REGULAR((max(plane.bit_length() - 2, 2),)),
    ]
    outs = (
        pltpu.VMEM(height.shape, f32),
        pltpu.VMEM(wind.shape, f32),
        pltpu.VMEM(moisture.shape, f32),
        pltpu.VMEM((1, size_x, size_y), f32),
        pltpu.VMEM((1, levels, coarse_x, coarse_y), f32),
        pltpu.VMEM(coeffs.shape, f32),
    )
    results = pl.pallas_call(
        functools.partial(kernel, sizes),
        out_shape=outs,
        in_specs=[pl.BlockSpec(memory_space=pltpu.HBM)] * 13,
        out_specs=(vmem,) * 6,
        scratch_shapes=scratch,
        compiler_params=pltpu.CompilerParams(
            collective_id=0, has_side_effects=True, vmem_limit_bytes=36 * 1024 * 1024
        ),
    )(*[pltpu.with_memory_space_constraint(a, pltpu.HBM) for a in operands])
    return pl.pallas_call(
        write_out,
        out_shape=tuple(jax.ShapeDtypeStruct(r.shape, f32) for r in results),
        in_specs=[vmem] * 6,
        out_specs=(pl.BlockSpec(memory_space=pl.ANY),) * 6,
        scratch_shapes=[dma((6,))],
        compiler_params=pltpu.CompilerParams(vmem_limit_bytes=8 * 1024 * 1024),
    )(*results)


def solution(mesh):
    sizes = (mesh.shape["mem"], mesh.shape["gx"], mesh.shape["gy"])
    in_specs = (
        P("mem", None, "gx", "gy"),
        P("mem", None, None, "gx", "gy"),
        P("mem", None, "gx", "gy"),
        P("mem", None, None, ("gx", "gy")),
        P(("gx", "gy")),
        P(),
        P(("gx", "gy"), None),
        P(),
        P(),
        P(),
        P(),
        P(),
        P(),
    )
    out_specs = (
        P("mem", None, "gx", "gy"),
        P("mem", None, None, "gx", "gy"),
        P("mem", None, "gx", "gy"),
        P("mem", "gx", "gy"),
        P("mem", None, None, None),
        P("mem", None, None, ("gx", "gy")),
    )
    return jax.shard_map(
        functools.partial(body, sizes),
        mesh=mesh,
        in_specs=in_specs,
        out_specs=out_specs,
        check_vma=False,
    )
```

```python
import functools

import jax
import jax.numpy as jnp
from jax import lax
from jax.experimental import pallas as pl
from jax.experimental.pallas import tpu as pltpu
from jax.sharding import PartitionSpec as P

RATIO = 8
ACOUSTIC = 2
HALO = 8
SPLIT = 2

acoustic_substep = 0.2
drift_step = 0.4

MESH = pl.DeviceIdType.MESH


def kernel(
    sizes,
    height,
    wind,
    moisture,
    coeffs_hbm,
    damping_hbm,
    vmix_hbm,
    basis_hbm,
    edge_source_hbm,
    row_cell_hbm,
    col_cell_hbm,
    cond_rate_hbm,
    saturation_hbm,
    ancestry_hbm,
    height_out,
    wind_out,
    moisture_out,
    rain_out,
    coarse_out,
    coeffs_out,
    coeffs,
    damping,
    vmix,
    basis,
    edge_source,
    row_cell,
    col_cell,
    cond_rate,
    saturation,
    ancestry,
    st,
    cf,
    st_sel,
    cf_sel,
    st_relay,
    cur,
    rows_out,
    rows_in,
    packed,
    packed_in,
    diag_in,
    rim_part,
    rim_in,
    rim_z,
    rim_full,
    table,
    sides,
    sides_t,
    spread,
    row_table3,
    coarse_rows_buf,
    coarse_part,
    coarse_in,
    halo_recv,
    batch,
    mem_send,
    mem_recv,
    local,
    rounds,
):
    members, count_x, count_y = sizes
    plane = count_x * count_y
    levels = cur.shape[0]
    size_x = st.shape[2]
    size_y = st.shape[3]
    full_x = row_cell.shape[1]
    full_y = col_cell.shape[1]
    rim_points = basis.shape[1]
    coarse_x = coarse_out.shape[2]
    coarse_y = coarse_out.shape[3]
    share = rim_part.shape[1]
    f32 = jnp.float32

    z = lax.axis_index("mem")
    ix = lax.axis_index("gx")
    iy = lax.axis_index("gy")
    here = ix * count_y + iy
    low_side = z < 2
    inner = jnp.logical_and(z > 0, z < members - 1)
    outer = jnp.logical_not(inner)
    near = jnp.where(low_side, 1 - z, 5 - z)
    cross_inner = jnp.where(low_side, 2, 1)
    cross_outer = jnp.where(low_side, 3, 0)

    def plane_peer(step):
        other = lax.rem(here + step, plane)
        return other, other // count_y, lax.rem(other, count_y)

    own_slots = pl.ds(z * levels, levels)
    loads = [
        (height.at[0], st.at[own_slots, 0]),
        (wind.at[0, 0], st.at[own_slots, 1]),
        (wind.at[0, 1], st.at[own_slots, 2]),
        (moisture.at[0], st.at[own_slots, 3]),
        (coeffs_hbm, coeffs),
        (damping_hbm, damping),
        (vmix_hbm, vmix),
        (basis_hbm, basis),
        (edge_source_hbm, edge_source),
        (row_cell_hbm, row_cell),
        (col_cell_hbm, col_cell),
        (cond_rate_hbm, cond_rate),
        (saturation_hbm, saturation),
        (ancestry_hbm, ancestry),
    ]
    copies = [pltpu.make_async_copy(a, b, local.at[n]) for n, (a, b) in enumerate(loads)]
    for copy in copies:
        copy.start()

    def ready(*which):
        for n in which:
            copies[n].wait()

    if plane & (plane - 1):
        steps = [lax.rem(here + step, plane) for step in range(1, plane)]
        n_rounds = 2
    else:
        n_dims = plane.bit_length() - 1
        n_rounds = max(n_dims - 1, 2)
        steps = []
        for k in range(n_dims):
            bit = lax.rem(here // 2**k, 2)
            steps.append(here + 2**k * (1 - 2 * bit))

    def greet(sem, n):
        for other in steps:
            pl.semaphore_signal(
                sem,
                inc=1,
                device_id=(z, other // count_y, lax.rem(other, count_y)),
                device_id_type=MESH,
            )
        pl.semaphore_signal(sem, inc=1, device_id=(near, ix, iy), device_id_type=MESH)

        @pl.when(inner)
        def _():
            for other in (cross_inner, cross_outer)[:n]:
                pl.semaphore_signal(
                    sem, inc=1, device_id=(other, ix, iy), device_id_type=MESH
                )

    barrier = pltpu.get_barrier_semaphore()
    greet(barrier, 2)

    ready(0, 1, 2, 3)

    pl.semaphore_wait(barrier, len(steps) + 2)
    greet(rounds.at[0], 1)

    pieces = [(0, pl.ds(0, 4)), (1, pl.ds(0, 2)), (1, pl.ds(2, 2))]
    pieces += [(l, pl.ds(0, 4)) for l in range(2, levels)]
    n_pieces = len(pieces)

    def chunk(c, slot):
        if c >= n_pieces:
            return cf.at[slot * 2 + c - n_pieces]
        return st.at[slot * levels + pieces[c][0], pieces[c][1]]

    def chosen(c, way):
        if c >= n_pieces:
            return cf_sel.at[way, c - n_pieces]
        return st_sel.at[way, pieces[c][0], pieces[c][1]]

    def z_copy(c, kind, src, slot, target):
        return pltpu.make_async_remote_copy(
            src_ref=src,
            dst_ref=chunk(c, slot),
            send_sem=mem_send.at[0 if c < n_pieces else 1],
            recv_sem=mem_recv.at[kind if c == 0 else 1 + 2 * c + kind],
            device_id=(target, ix, iy),
            device_id_type=MESH,
        )

    def own_near(c):
        return z_copy(c, 0, chunk(c, z), z, near)

    def own_cross(c):
        return z_copy(c, jnp.where(outer, 2, 1), chunk(c, z), z, cross_inner)

    def sel_inner(c):
        return z_copy(c, 1, chosen(c, 0), z, cross_inner)

    def sel_outer(c):
        return z_copy(c, 1, chosen(c, 1), z, cross_outer)

    def relay_near(c):
        return z_copy(c, 0, st_relay, z, near)

    def arrived(c, kind, slot):
        z_copy(c, kind, chunk(c, slot), slot, near).wait_recv()

    first, rest = 0, list(range(1, n_pieces))
    specs = [n_pieces, n_pieces + 1]
    lead, later = rest[:2], rest[2:]

    @pl.when(inner)
    def _():
        own_cross(first).start()
        for c in rest:
            own_near(c).start()

    @pl.when(outer)
    def _():
        for c in lead:
            own_near(c).start()
        own_cross(first).start()
        for c in later:
            own_near(c).start()

    ready(4, 5, 6)
    new_fields = []
    for f in range(4):
        c = coeffs[0, f]
        acc = vmix[:, 0:1] * c[0:1]
        for j in range(1, levels):
            acc = acc + vmix[:, j : j + 1] * c[j : j + 1]
        new_fields.append(acc * damping[...])
    for f in range(4):
        cf[2 * z + f // 2, f % 2] = new_fields[f]
    pl.semaphore_wait(rounds.at[0], len(steps) + jnp.where(inner, 2, 1))
    for k in range(1, n_rounds):
        greet(rounds.at[k], 0)
        if k < n_rounds - 1:
            pl.semaphore_wait(rounds.at[k], len(steps) + 1)
    low = jnp.concatenate(new_fields, axis=0).astype(jnp.bfloat16)
    ready(7)
    part = jnp.dot(low, basis[...], preferred_element_type=f32)
    for g in range(count_x):
        rim_part[g] = part[g * share : (g + 1) * share]

    def rim_copy(step):
        _, px, py = plane_peer(step)
        return pltpu.make_async_remote_copy(
            src_ref=rim_part.at[px],
            dst_ref=rim_in.at[here],
            send_sem=batch.at[0],
            recv_sem=batch.at[1],
            device_id=(z, px, py),
            device_id_type=MESH,
        )

    pl.semaphore_wait(rounds.at[n_rounds - 1], len(steps) + 1)
    for step in range(1, plane):
        rim_copy(step).start()

    ready(8, 9, 10, 11, 12, 13)
    mine = ancestry[z]

    def select_near(c):
        arrived(c, 0, near)
        for way, target in ((0, cross_inner), (1, cross_outer)):
            take_own = ancestry[target] != near
            chosen(c, way)[...] = jnp.where(take_own, chunk(c, z)[...], chunk(c, near)[...])

    n_edge = edge_source.shape[0]
    table[...] = (
        (lax.broadcasted_iota(jnp.int32, (rim_points, n_edge), 0)
         == edge_source[...].reshape(1, n_edge))
        .astype(f32)
        .astype(jnp.bfloat16)
    )
    row_table = (
        lax.broadcasted_iota(jnp.int32, (coarse_x, full_x), 0) == row_cell[...]
    ).astype(f32)
    row_count = jnp.sum(row_table, axis=1, keepdims=True)
    wide = lax.rem(
        lax.broadcasted_iota(jnp.int32, (levels * coarse_y, full_y), 0), coarse_y
    )
    col_table = (wide == col_cell[...]).astype(f32)
    col_count = lax.dot_general(
        jnp.ones((8, full_y), f32),
        col_table,
        (((1,), (1,)), ((), ())),
        preferred_element_type=f32,
    )[0:1]
    col_off = pl.multiple_of(iy * size_y, 128)
    row_off = pl.multiple_of(ix * size_x, 8)
    cells_here = col_cell[:, pl.ds(col_off, size_y)]
    wide_here = lax.broadcasted_iota(jnp.int32, (levels * coarse_y, size_y), 0)
    coarse_rows_buf[...] = jnp.zeros_like(coarse_rows_buf)
    for m in range(3):
        row_table3[:, m * full_x : (m + 1) * full_x] = row_table.astype(jnp.bfloat16)

    @pl.when(inner)
    def _():
        for c in lead:
            select_near(c)
            sel_outer(c).start()
        for c in lead:
            sel_inner(c).start()

    def batch_of(n, ref, count):
        many = ref.at[pl.ds(0, count)]
        return pltpu.make_async_remote_copy(
            src_ref=many,
            dst_ref=many,
            send_sem=batch.at[n],
            recv_sem=batch.at[n + 1],
            device_id=(near, ix, iy),
            device_id_type=MESH,
        )

    batch_of(0, rim_in, plane - 1).wait_recv()
    total = rim_part[ix]
    for step in range(1, plane):
        other, _, _ = plane_peer(step)
        total = total + rim_in[other]
    rim_z[z] = total

    def rimz_copy(step, source):
        return pltpu.make_async_remote_copy(
            src_ref=rim_z.at[source],
            dst_ref=rim_z.at[source],
            send_sem=batch.at[2],
            recv_sem=batch.at[3],
            device_id=(lax.rem(z + step, members), ix, iy),
            device_id_type=MESH,
        )

    for step in range(1, members):
        rimz_copy(step, z).start()

    @pl.when(outer)
    def _():
        for c in [first] + specs:
            own_near(c).start()

    @pl.when(inner)
    def _():
        arrived(first, 1, cross_inner)
        arrived(first, 2, cross_outer)
        want = ancestry[near]
        a = chunk(first, z)[...]
        a = jnp.where(want == cross_inner, chunk(first, cross_inner)[...], a)
        st_relay[...] = jnp.where(want == cross_outer, chunk(first, cross_outer)[...], a)
        relay_near(first).start()
        for c in later:
            select_near(c)
            sel_outer(c).start()
        for c in later:
            sel_inner(c).start()

    batch_of(2, rim_z, members - 1).wait_recv()
    share_sel = rim_z[z]
    for step in range(1, members):
        source = lax.rem(z + step, members)
        share_sel = jnp.where(mine == source, rim_z[source], share_sel)
    rim_full[ix] = share_sel

    def rimg_copy(step, source):
        return pltpu.make_async_remote_copy(
            src_ref=rim_full.at[source],
            dst_ref=rim_full.at[source],
            send_sem=batch.at[4],
            recv_sem=batch.at[5],
            device_id=(z, lax.rem(ix + step, count_x), iy),
            device_id_type=MESH,
        )

    for step in range(1, count_x):
        rimg_copy(step, ix).start()

    @pl.when(inner)
    def _():
        arrived(first, 0, near)
        for c in specs:
            own_near(c).start()

    lane = lax.broadcasted_iota(jnp.int32, (size_x, size_y), 1)
    width = size_y // (4 * levels)
    half = width // 2

    def settle(c, ref):
        arrived(c, 1, cross_inner)

        @pl.when(outer)
        def _():
            arrived(c, 0, near)

        a = jnp.where(mine == z, chunk(c, z)[...], chunk(c, cross_inner)[...])
        ref[...] = jnp.where(mine == near, chunk(c, near)[...], a)

    order = list(range(1, levels - 1)) + [first, levels - 1]
    groups = [order[:SPLIT], order[SPLIT:]]
    for n, l in enumerate(order):
        hit = ((wide_here - l * coarse_y) == cells_here).astype(f32).astype(jnp.bfloat16)
        for m in range(3):
            spread[:, (3 * n + m) * size_y : (3 * n + m + 1) * size_y] = hit

    def halo_jobs(g, mode):
        lev = pl.ds(SPLIT * g, len(groups[g]))
        toward = [(-1, -1), (0, -1), (-1, 0), (1, -1), (-1, 1), (0, 1), (1, 1), (1, 0)]
        for dx, dy in toward:
            if True:
                flip = -1 if mode == "recv" else 1
                ok = jnp.bool_(True)
                if dx * flip == -1:
                    ok = jnp.logical_and(ok, ix > 0)
                if dx * flip == 1:
                    ok = jnp.logical_and(ok, ix < count_x - 1)
                if dy * flip == -1:
                    ok = jnp.logical_and(ok, iy > 0)
                if dy * flip == 1:
                    ok = jnp.logical_and(ok, iy < count_y - 1)
                sx = 0 if dx == -1 else 1
                sy = 0 if dy == -1 else 1
                rows = pl.ds(0, HALO) if dx == -1 else pl.ds(size_x // 2 - HALO, HALO)
                if dy == 0:
                    src, dst, base = rows_out.at[sx, lev], rows_in.at[sx, lev], sx
                elif dx == 0:
                    src, dst, base = packed.at[g], packed_in.at[g, sy], 2 + sy
                else:
                    src, dst = packed.at[g, rows, :], diag_in.at[g, sx, sy]
                    base = 4 + 2 * sx + sy

                def go(src=src, dst=dst, base=base, target=(z, ix + dx, iy + dy)):
                    copy = pltpu.make_async_remote_copy(
                        src_ref=src,
                        dst_ref=dst,
                        send_sem=local.at[8 * g + base],
                        recv_sem=halo_recv.at[8 * g + base],
                        device_id=target,
                        device_id_type=MESH,
                    )
                    if mode == "start":
                        copy.start()
                    elif mode == "send":
                        copy.wait_send()
                    else:
                        copy.wait_recv()

                pl.when(ok)(go)

    fold = size_x // 2

    def halo_out(g):
        pack = jnp.zeros((size_x, size_y), f32)
        for l in groups[g]:
            if l != first:
                for c in range(n_pieces):
                    if pieces[c][0] == l:
                        settle(c, cur.at[l, pieces[c][1]])
            for f in range(4):
                rows_out[0, order.index(l), f] = cur[l, f, 0:HALO]
                rows_out[1, order.index(l), f] = cur[l, f, size_x - HALO :]
                k = f * len(groups[g]) + groups[g].index(l)
                moved = pltpu.roll(cur[l, f], (width * k + half) % size_y, 1)
                pack = jnp.where(lane // width == k, moved, pack)
        below_half = pltpu.roll(pack[fold:], size_y // 2, 1)
        packed[g] = jnp.where(lane[:fold] < size_y // 2, pack[:fold], below_half)
        halo_jobs(g, "start")

    halo_out(0)

    @pl.when(inner)
    def _():
        for c in specs:
            select_near(c)
            sel_outer(c).start()
        for c in specs:
            sel_inner(c).start()

    @pl.when(outer)
    def _():
        arrived(first, 0, near)
        cur[first] = jnp.where(mine == z, chunk(first, z)[...], chunk(first, near)[...])

    @pl.when(inner)
    def _():
        a = chunk(first, cross_outer)[...]
        a = jnp.where(mine == cross_inner, chunk(first, cross_inner)[...], a)
        a = jnp.where(mine == near, chunk(first, near)[...], a)
        cur[first] = jnp.where(mine == z, chunk(first, z)[...], a)

    halo_out(1)

    ext_x = size_x + 2 * HALO
    ext_y = 2 * size_y
    rpos = lax.broadcasted_iota(jnp.int32, (ext_x, ext_y), 0)
    cpos = lax.broadcasted_iota(jnp.int32, (ext_x, ext_y), 1)
    gx_pos = ix * size_x + jnp.where(rpos < size_x + HALO, rpos, rpos - ext_x)
    gy_pos = iy * size_y + jnp.where(cpos < size_y + size_y // 2, cpos, cpos - ext_y)
    beside = slice(size_y, ext_y)
    above = slice(size_x, size_x + HALO)
    below = slice(size_x + HALO, ext_x)
    has_up = ix < count_x - 1
    has_down = ix > 0

    def inside(rows):
        xs, ys = gx_pos[rows, beside], gy_pos[rows, beside]
        return (xs >= 0) & (xs < full_x) & (ys >= 0) & (ys < full_y)

    in_main, in_up, in_down = inside(slice(0, size_x)), inside(above), inside(below)

    batch_of(4, rim_full, count_x - 1).wait_recv()
    rim = jnp.concatenate([rim_full[g] for g in range(count_x)], axis=0)
    rim_hi = rim.astype(jnp.bfloat16)
    rim_lo = (rim - rim_hi.astype(f32)).astype(jnp.bfloat16)
    both = jnp.dot(
        jnp.concatenate([rim_hi, rim_lo], axis=0), table[...], preferred_element_type=f32
    )
    n_rows = 4 * levels
    edge = both[0:n_rows] + both[n_rows:]
    sides[...] = edge
    for s in range(2):
        begin = 2 * full_y + s * full_x
        sides_t[s, HALO : HALO + full_x, :] = edge[:, begin : begin + full_x].T
        sides_t[s, 0:HALO, :] = jnp.zeros((HALO, n_rows), f32)
        sides_t[s, HALO + full_x :, :] = jnp.zeros((HALO, n_rows), f32)
    lane1 = lax.broadcasted_iota(jnp.int32, (n_rows, size_y), 1)

    def x_side(begin):
        own = sides[:, pl.ds(pl.multiple_of(begin + col_off, 128), size_y)]
        after = lax.rem(iy + 1, count_y) * size_y
        before = lax.rem(iy + count_y - 1, count_y) * size_y
        nxt_b = sides[:, pl.ds(pl.multiple_of(begin + after, 128), size_y)]
        prv_b = sides[:, pl.ds(pl.multiple_of(begin + before, 128), size_y)]
        return jnp.concatenate([own, jnp.where(lane1 < size_y // 2, nxt_b, prv_b)], axis=1)

    def y_side(s):
        body_rows = sides_t[s, pl.ds(pl.multiple_of(row_off + HALO, 8), size_x), :]
        above = sides_t[s, pl.ds(pl.multiple_of(row_off + HALO + size_x, 8), HALO), :]
        below = sides_t[s, pl.ds(row_off, HALO), :]
        return jnp.concatenate([body_rows, above, below], axis=0)

    west, east = x_side(0), x_side(full_y)
    south, north = y_side(0), y_side(1)
    if count_y > 1:
        column = jnp.where(iy == 0, south, north)

    lane2 = lax.broadcasted_iota(jnp.int32, (size_x + 2 * HALO, size_y), 1)
    take_next = lax.rem(lane2, width) >= half
    rains = {}
    thirds = []
    summed = jnp.zeros((size_x, levels * coarse_y), f32)

    def split(a):
        parts = []
        for _ in range(3):
            parts.append(a.astype(jnp.bfloat16))
            a = a - parts[-1].astype(f32)
        return parts

    for l in order:
        at = order.index(l)
        g = at // SPLIT
        if l == groups[g][0]:
            halo_jobs(g, "recv")


            def unfold(way):
                part = packed_in[g, way]
                turned = pltpu.roll(part, size_y // 2, 1)
                corner = pltpu.roll(diag_in[g, 1, way], size_y // 2, 1)
                return jnp.concatenate([part, turned, diag_in[g, 0, way], corner], axis=0)

            mixed = jnp.where(take_next, unfold(0), unfold(1))

        def extended(f):
            k = f * len(groups[g]) + groups[g].index(l)
            left = jnp.concatenate([cur[l, f], rows_in[0, at, f], rows_in[1, at, f]], axis=0)
            right = pltpu.roll(mixed, (size_y - (width * k + half)) % size_y, 1)
            return jnp.concatenate([left, right], axis=1)

        def frame(f):
            k = f * levels + l
            if count_y > 1:
                side = jnp.broadcast_to(column[:, k : k + 1], (ext_x, size_y))
            else:
                at_south = gy_pos[:, beside] < 0
                side = jnp.where(at_south, south[:, k : k + 1], north[:, k : k + 1])
            eastern = jnp.broadcast_to(east[k : k + 1], (HALO, ext_y))
            western = jnp.broadcast_to(west[k : k + 1], (HALO, ext_y))
            up_v = jnp.where(has_up, side[above], eastern[:, beside])
            down_v = jnp.where(has_down, side[below], western[:, beside])

            def put(a):
                left = jnp.concatenate(
                    [
                        a[0:size_x, 0:size_y],
                        jnp.where(has_up, a[above, 0:size_y], eastern[:, 0:size_y]),
                        jnp.where(has_down, a[below, 0:size_y], western[:, 0:size_y]),
                    ],
                    axis=0,
                )
                right = jnp.concatenate(
                    [
                        jnp.where(in_main, a[0:size_x, beside], side[0:size_x]),
                        jnp.where(in_up, a[above, beside], up_v),
                        jnp.where(in_down, a[below, beside], down_v),
                    ],
                    axis=0,
                )
                return jnp.concatenate([left, right], axis=1)

            return put

        def up(a):
            return pltpu.roll(a, ext_x - 1, 0)

        def down(a):
            return pltpu.roll(a, 1, 0)

        def right_of(a):
            return pltpu.roll(a, ext_y - 1, 1)

        def left_of(a):
            return pltpu.roll(a, 1, 1)

        put_h, put_u, put_v, put_q = frame(0), frame(1), frame(2), frame(3)
        h, u, v, q = extended(0), extended(1), extended(2), extended(3)
        h = put_h(h)
        q = put_q(q)
        for substep in range(ACOUSTIC):
            u = u - acoustic_substep * (up(h) - down(h))
            v = v - acoustic_substep * (right_of(h) - left_of(h))
            u = put_u(u)
            v = put_v(v)
            h = h - acoustic_substep * ((up(u) - down(u)) + (right_of(v) - left_of(v)))
            h = put_h(h)
        flux = (
            jnp.maximum(u, 0.0) * (q - down(q)) + jnp.minimum(u, 0.0) * (up(q) - q)
        ) + (
            jnp.maximum(v, 0.0) * (q - left_of(q)) + jnp.minimum(v, 0.0) * (right_of(q) - q)
        )
        q = (q - drift_step * flux)[0:size_x, 0:size_y]
        fallen = cond_rate[l] * jnp.maximum(q - saturation[l], 0.0)
        q_new = q - fallen
        height_out[0, l] = h[0:size_x, 0:size_y]
        wind_out[0, 0, l] = u[0:size_x, 0:size_y]
        wind_out[0, 1, l] = v[0:size_x, 0:size_y]
        moisture_out[0, l] = q_new
        rains[l] = fallen
        thirds += split(q_new)
        if l == groups[g][-1]:
            span = spread[:, 3 * size_y * (at + 1 - len(groups[g])) : 3 * size_y * (at + 1)]
            summed = summed + lax.dot_general(
                jnp.concatenate(thirds, axis=1),
                span,
                (((1,), (1,)), ((), ())),
                preferred_element_type=f32,
            )
            thirds = []

    for n, third in enumerate(split(summed)):
        start = pl.multiple_of(n * full_x + row_off, 16)
        coarse_rows_buf[pl.ds(start, size_x), :] = third
    coarse_part[...] = jnp.dot(
        row_table3[...], coarse_rows_buf[...], preferred_element_type=f32
    )

    def crs_copy(other):
        px, py = other // count_y, other % count_y
        return pltpu.make_async_remote_copy(
            src_ref=coarse_part,
            dst_ref=coarse_in.at[here],
            send_sem=batch.at[6],
            recv_sem=batch.at[7],
            device_id=(z, px, py),
            device_id_type=MESH,
        )

    for other in range(plane):
        pl.when(here != other)(crs_copy(other).start)
    rain = rains[0]
    for l in range(1, levels):
        rain = rain + rains[l]
    rain_out[0] = rain

    for half_at, c in enumerate(specs):
        settle(c, coeffs_out.at[0, pl.ds(2 * half_at, 2)])

    for g in range(2):
        halo_jobs(g, "send")
    batch_of(0, rim_in, plane - 1).wait_send()
    batch_of(2, rim_z, members - 1).wait_send()
    batch_of(4, rim_full, count_x - 1).wait_send()

    def sent(n, ref, count):
        many = ref.at[pl.ds(0, count)]
        pltpu.make_async_remote_copy(
            src_ref=many,
            dst_ref=many,
            send_sem=mem_send.at[n],
            recv_sem=mem_recv.at[0],
            device_id=(near, ix, iy),
            device_id_type=MESH,
        ).wait_send()

    @pl.when(outer)
    def _():
        sent(0, st, levels + 1)
        sent(1, cf, 2)

    @pl.when(inner)
    def _():
        sent(0, st, 3 * levels - 1)
        sent(1, cf, 6)

    batch_of(6, coarse_in, plane - 1).wait_recv()
    total = coarse_part[...]
    for step in range(1, plane):
        other, _, _ = plane_peer(step)
        total = total + coarse_in[other]
    total = total / (row_count * col_count)
    for l in range(levels):
        coarse_out[0, l] = total[:, l * coarse_y : (l + 1) * coarse_y]

    batch_of(6, coarse_in, plane - 1).wait_send()


def write_out(*refs):
    sems = refs[12]
    copies = [pltpu.make_async_copy(refs[n], refs[6 + n], sems.at[n]) for n in range(6)]
    for copy in copies:
        copy.start()
    for copy in copies:
        copy.wait()


def body(
    sizes,
    height,
    wind,
    moisture,
    coeffs,
    damping,
    vmix,
    basis,
    edge_source,
    row_cell,
    col_cell,
    cond_rate,
    saturation,
    ancestry,
):
    members, count_x, count_y = sizes
    plane = count_x * count_y
    _, levels, size_x, size_y = height.shape
    local_k = coeffs.shape[3]
    rim_points = basis.shape[1]
    full_x = row_cell.shape[0]
    full_y = col_cell.shape[0]
    n_edge = edge_source.shape[0]
    coarse_x, coarse_y = full_x // RATIO, full_y // RATIO
    share = 4 * levels // count_x
    rows = 4 * levels
    f32 = jnp.float32
    vmem = pl.BlockSpec(memory_space=pltpu.VMEM)
    dma = pltpu.SemaphoreType.DMA
    coarse_chunk = (coarse_x, levels * coarse_y)
    operands = (
        height,
        wind,
        moisture,
        coeffs,
        damping.reshape(1, -1),
        vmix,
        basis,
        edge_source,
        row_cell.reshape(1, -1),
        col_cell.reshape(1, -1),
        cond_rate,
        saturation,
        ancestry,
    )
    chunks = levels + 3
    scratch = [
        *[pltpu.VMEM(a.shape, a.dtype) for a in operands[3:10]],
        *[pltpu.SMEM(a.shape, a.dtype) for a in operands[10:]],
        pltpu.VMEM((members * levels, 4, size_x, size_y), f32),
        pltpu.VMEM((members * 2, 2, levels, local_k), f32),
        pltpu.VMEM((2, levels, 4, size_x, size_y), f32),
        pltpu.VMEM((2, 2, 2, levels, local_k), f32),
        pltpu.VMEM((4, size_x, size_y), f32),
        pltpu.VMEM((levels, 4, size_x, size_y), f32),
        pltpu.VMEM((2, levels, 4, HALO, size_y), f32),
        pltpu.VMEM((2, levels, 4, HALO, size_y), f32),
        pltpu.VMEM((2, size_x // 2, size_y), f32),
        pltpu.VMEM((2, 2, size_x // 2, size_y), f32),
        pltpu.VMEM((2, 2, 2, HALO, size_y), f32),
        pltpu.VMEM((count_x, share, rim_points), f32),
        pltpu.VMEM((plane, share, rim_points), f32),
        pltpu.VMEM((members, share, rim_points), f32),
        pltpu.VMEM((count_x, share, rim_points), f32),
        pltpu.VMEM((rim_points, n_edge), jnp.bfloat16),
        pltpu.VMEM((rows, n_edge), f32),
        pltpu.VMEM((2, full_x + 2 * HALO, rows), f32),
        pltpu.VMEM((levels * coarse_y, 3 * levels * size_y), jnp.bfloat16),
        pltpu.VMEM((coarse_x, 3 * full_x), jnp.bfloat16),
        pltpu.VMEM((3 * full_x, levels * coarse_y), jnp.bfloat16),
        pltpu.VMEM(coarse_chunk, f32),
        pltpu.VMEM((plane, *coarse_chunk), f32),
        dma((16,)),
        dma((8,)),
        dma((2,)),
        dma((1 + 2 * chunks,)),
        dma((16,)),
        pltpu.SemaphoreType.REGULAR((max(plane.bit_length() - 2, 2),)),
    ]
    outs = (
        pltpu.VMEM(height.shape, f32),
        pltpu.VMEM(wind.shape, f32),
        pltpu.VMEM(moisture.shape, f32),
        pltpu.VMEM((1, size_x, size_y), f32),
        pltpu.VMEM((1, levels, coarse_x, coarse_y), f32),
        pltpu.VMEM(coeffs.shape, f32),
    )
    results = pl.pallas_call(
        functools.partial(kernel, sizes),
        out_shape=outs,
        in_specs=[pl.BlockSpec(memory_space=pltpu.HBM)] * 13,
        out_specs=(vmem,) * 6,
        scratch_shapes=scratch,
        compiler_params=pltpu.CompilerParams(
            collective_id=0, has_side_effects=True, vmem_limit_bytes=36 * 1024 * 1024
        ),
    )(*[pltpu.with_memory_space_constraint(a, pltpu.HBM) for a in operands])
    return pl.pallas_call(
        write_out,
        out_shape=tuple(jax.ShapeDtypeStruct(r.shape, f32) for r in results),
        in_specs=[vmem] * 6,
        out_specs=(pl.BlockSpec(memory_space=pl.ANY),) * 6,
        scratch_shapes=[dma((6,))],
        compiler_params=pltpu.CompilerParams(vmem_limit_bytes=8 * 1024 * 1024),
    )(*results)


def solution(mesh):
    sizes = (mesh.shape["mem"], mesh.shape["gx"], mesh.shape["gy"])
    in_specs = (
        P("mem", None, "gx", "gy"),
        P("mem", None, None, "gx", "gy"),
        P("mem", None, "gx", "gy"),
        P("mem", None, None, ("gx", "gy")),
        P(("gx", "gy")),
        P(),
        P(("gx", "gy"), None),
        P(),
        P(),
        P(),
        P(),
        P(),
        P(),
    )
    out_specs = (
        P("mem", None, "gx", "gy"),
        P("mem", None, None, "gx", "gy"),
        P("mem", None, "gx", "gy"),
        P("mem", "gx", "gy"),
        P("mem", None, None, None),
        P("mem", None, None, ("gx", "gy")),
    )
    return jax.shard_map(
        functools.partial(body, sizes),
        mesh=mesh,
        in_specs=in_specs,
        out_specs=out_specs,
        check_vma=False,
    )
```
